256 devices in a mesh: row: 16 (over x_hi, z), col: 16 (over y, x_lo, core).
Axes of the slice: x: 4 (x_hi: 2, x_lo: 2; x = x_hi * 2 + x_lo), y: 4, z: 8, core: 2. Of those that a mesh axis runs over, the one named last changes fastest.
Arguments:
- charges: bfloat16 [2097152], P(('row', 'col')), may hold values from -6 to 6
- panel_order: int32 [2097152], P(('row', 'col')), may hold values from 0 to 8191, as said below
- patch_anchor: int32 [3, 32768], P(None, ('row', 'col')), may hold values from 0 to 252, as said below
- project: bfloat16 [32768, 4096], P(('row', 'col')), may hold values from -0.75 to 0.75
- interpolate: bfloat16 [32768, 4096], P(('row', 'col')), may hold values from -0.75 to 0.75
- kernel_spectrum: float32 [512, 512, 512], P('row', 'col'), may hold values from 0.5 to 8
- near_pairs: int32 [2, 131072], P(None, ('row', 'col')), may hold values from 0 to 32767, as said below
- near_blocks: bfloat16 [131072, 4096], P(('row', 'col')), may hold values from -0.75 to 0.75
Outputs:
- potential: float32 [2097152], P(('row', 'col'))
The draws below stay inside these ranges and needn't reach their ends.
Inputs may be any that keep to these rules, and one draw needn't show every extreme that they name: `panel_order`: the entries of each aligned run of 8192 slots (one device's slots) are a permutation of 0 to 8191. `patch_anchor`: block b lies on device d = b // 128 at row index r = d // 16 and col index c = d % 16; its first coordinate lies in r * 16 to (r + 1) * 16 - 1, its second in c * 16 to (c + 1) * 16 - 1, and all three coordinates are at most 252. `near_pairs`: the pairs on a device have that device's blocks as targets, each block exactly 4 times; each source block lies on the same device or on one whose row and col indices each differ by at most one.
All inputs are finite; a program needn't handle non-finite values.
Results may differ from the reference program's by a relative error of at most 0.0025.
Values may be sent and summed in bfloat16 or wider, within the bound.
A program may use at most 128 MiB of HBM per device.

```python
import math
import jax
import jax.numpy as jnp
from jax import lax

G = 256
P_SIZE = 512
BLK = 64
PTS = 64
NB = 128
NEAR = 4
CX = 16
CY = 16
BLOCKS = 32768
PANELS = 2097152
PAIRS = 131072
DEVICES = 256


def draw_panel_order(key, part):
    keys = jax.random.split(jax.random.fold_in(key, 11), DEVICES)
    orders = jax.vmap(lambda one: jax.random.permutation(one, NB * BLK))(keys).astype(jnp.int32)
    return orders.reshape(PANELS)


def draw_patch_anchor(key, part):
    mesh_cols = G // CY
    index = jnp.arange(BLOCKS, dtype=jnp.int32)
    device = index // NB
    local = index % NB
    row_at = device // mesh_cols
    col_at = device % mesh_cols

    def along(salt, start, cells):
        upper = jnp.minimum(start + cells, G - 3)
        raw = jax.random.randint(jax.random.fold_in(key, salt), (BLOCKS,), 0, 1 << 20)
        picked = start + raw % (upper - start)
        return jnp.where(local == 0, start, jnp.where(local == 1, upper - 1, picked))
    first = along(21, row_at * CX, CX)
    second = along(22, col_at * CY, CY)
    third = along(23, jnp.zeros_like(index), G)
    return jnp.stack([first, second, third]).astype(jnp.int32)


def draw_near_pairs(key, part):
    mesh_rows = G // CX
    mesh_cols = G // CY
    index = jnp.arange(PAIRS, dtype=jnp.int32)
    device = index // (NEAR * NB)
    target = device * NB + index % (NEAR * NB) % NB
    row_at = device // mesh_cols
    col_at = device % mesh_cols
    step_row = jax.random.randint(jax.random.fold_in(key, 31), (PAIRS,), -1, 2)
    step_col = jax.random.randint(jax.random.fold_in(key, 32), (PAIRS,), -1, 2)
    local = jax.random.randint(jax.random.fold_in(key, 33), (PAIRS,), 0, NB)
    source_row = jnp.clip(row_at + step_row, 0, mesh_rows - 1)
    source_col = jnp.clip(col_at + step_col, 0, mesh_cols - 1)
    source = (source_row * mesh_cols + source_col) * NB + local
    return jnp.stack([target, source]).astype(jnp.int32)


def block_levels(own_key, dims, shards, least, top_value):
    gain, own = 1.0, jax.random.fold_in(own_key, 6)
    for position, shards_of in shards:
        heights = jnp.exp(jax.random.uniform(jax.random.fold_in(own, position), (shards_of,), jnp.float32, least / len(shards), top_value / len(shards)))
        gain = gain * jnp.repeat(heights, dims[position] // shards_of).reshape([-1 if axis == position else 1 for axis in range(len(dims))])
    return gain


def scatter_about(key, extent, scale, reach, pieces=(), held_as=jnp.bfloat16):
    loudness = block_levels(key, extent, pieces, -0.22, 0.18) if pieces else 1.0
    values = jax.random.normal(key, extent, jnp.float32) * scale * loudness
    return jnp.minimum(jnp.maximum(values, -reach), reach).astype(held_as)


def setup_inputs(seed: int = 0) -> dict:
    seeds = jax.random.split(jax.random.key(seed), 9)
    charges = scatter_about(seeds[0], (PANELS,), 1.0, 6.0, ((0, 256),))
    panel_order = draw_panel_order(jax.random.fold_in(seeds[8], 71), 0)
    patch_anchor = draw_patch_anchor(jax.random.fold_in(seeds[8], 71), 0)
    project = scatter_about(seeds[3], (BLOCKS, PTS * BLK), BLK ** -0.5, 0.75, ((0, 256),))
    interpolate = scatter_about(seeds[4], (BLOCKS, BLK * PTS), PTS ** -0.5, 0.75, ((0, 256),))
    kernel_spectrum = jnp.clip(jnp.exp(math.log(8.0) - 2.7725887 * jax.random.uniform(seeds[5], (P_SIZE, P_SIZE, P_SIZE), jnp.float32) ** block_levels(seeds[5], (P_SIZE, P_SIZE, P_SIZE), ((0, 16), (1, 16)), -0.2, 0.2)), 0.5, 8.0)
    near_pairs = draw_near_pairs(jax.random.fold_in(seeds[8], 71), 0)
    near_blocks = scatter_about(seeds[7], (PAIRS, BLK * BLK), BLK ** -0.5, 0.75, ((0, 256),))
    return dict(charges=charges, panel_order=panel_order, patch_anchor=patch_anchor, project=project, interpolate=interpolate, kernel_spectrum=kernel_spectrum, near_pairs=near_pairs, near_blocks=near_blocks)


def cas_table(rows, cols):
    first = jnp.arange(rows, dtype=jnp.int32)[:, None]
    second = jnp.arange(cols, dtype=jnp.int32)[None, :]
    phase = (first * second % P_SIZE).astype(jnp.float32) * (2.0 * math.pi / P_SIZE)
    return (jnp.cos(phase) + jnp.sin(phase)) / math.sqrt(P_SIZE)

def block_products(mats, vecs, rows_out):
    count = mats.shape[0] // NB
    cols_in = vecs.shape[1]

    def single(pair):
        shaped = pair[0].reshape(NB, rows_out, cols_in).astype(jnp.float32)
        return jnp.einsum('bij,bj->bi', shaped, pair[1].astype(jnp.float32))
    stacked = lax.map(single, (mats.reshape(count, NB, mats.shape[1]), vecs.reshape(count, NB, cols_in)))
    return stacked.reshape(mats.shape[0], rows_out)

def reference(charges, panel_order, patch_anchor, project, interpolate, kernel_spectrum, near_pairs, near_blocks):
    slots = jnp.arange(PANELS, dtype=jnp.int32)
    global_order = slots // (NB * BLK) * (NB * BLK) + panel_order
    block_charges = charges[global_order].reshape(BLOCKS, BLK)
    patch = block_products(project, block_charges, PTS)
    points = jnp.arange(PTS, dtype=jnp.int32)
    xs = patch_anchor[0][:, None] + (points // 16)[None, :]
    ys = patch_anchor[1][:, None] + (points // 4 % 4)[None, :]
    zs = patch_anchor[2][:, None] + (points % 4)[None, :]
    grid = jnp.zeros((G, G, G), jnp.float32).at[xs, ys, zs].add(patch)
    forward = cas_table(G, P_SIZE)
    backward = cas_table(P_SIZE, G)
    highest = lax.Precision.HIGHEST
    spec = jnp.einsum('xyz,zf->xyf', grid, forward, precision=highest)
    spec = jnp.einsum('xyf,yg->xgf', spec, forward, precision=highest)
    spec = jnp.einsum('xgf,xh->hgf', spec, forward, precision=highest)
    spec = spec * jnp.transpose(kernel_spectrum, (2, 0, 1))
    field = jnp.einsum('hgf,hx->xgf', spec, backward, precision=highest)
    field = jnp.einsum('xgf,gy->xyf', field, backward, precision=highest)
    field = jnp.einsum('xyf,fz->xyz', field, backward, precision=highest)
    values = field[xs, ys, zs].astype(jnp.bfloat16)
    far = block_products(interpolate, values, BLK)
    near_terms = block_products(near_blocks, block_charges[near_pairs[1]], BLK)
    near = jnp.zeros((BLOCKS, BLK), jnp.float32).at[near_pairs[0]].add(near_terms)
    return jnp.zeros((PANELS,), jnp.float32).at[global_order].set((far + near).reshape(PANELS))
```

```python
import math

import jax
import jax.numpy as jnp
import numpy as np
from jax import lax
from jax.experimental import pallas as pl
from jax.experimental.pallas import tpu as pltpu
from jax.sharding import PartitionSpec as P

G = 256
P_SIZE = 512
BLK = 64
PTS = 64
N = 16
OWN = 256
EXT = 368
CH = 4
F32 = jnp.float32
BF16 = jnp.bfloat16
LANES = 128
ROWS = 64
PICK = 384
I32 = jnp.int32
NEIGHBOURS = [(a, b) for a in (-1, 0, 1) for b in (-1, 0, 1) if (a, b) != (0, 0)]


def tables():
    first = np.arange(G)[:, None]
    second = np.arange(P_SIZE)[None, :]
    phase = (first * second % P_SIZE).astype(np.float64) * (2.0 * math.pi / P_SIZE)
    table = (np.cos(phase) + np.sin(phase)) / math.sqrt(P_SIZE)
    high = table.astype(BF16)
    low = (table - high.astype(np.float64)).astype(BF16)
    forward = np.stack([high, low])
    backward = np.stack([high.T, low.T])
    swap = np.zeros((P_SIZE, P_SIZE), np.float32)
    x, f = np.meshgrid(np.arange(16), np.arange(32), indexing="ij")
    swap[x * 32 + f, f * 16 + x] = 1.0
    swap = swap.astype(BF16)
    into = np.stack([swap[:, 128 * k : 128 * k + 128] for k in range(CH)])
    back = np.stack([swap.T[128 * k : 128 * k + 128, :] for k in range(CH)])
    return forward, backward, into, back


def transposed_groups(parts, lanes):
    count = len(parts)
    group = 128 // count
    distance = count // 2
    parts = list(parts)
    while distance:
        shift = distance * group
        upper = (lanes // shift) % 2 == 1
        for q in range(count):
            if q & distance:
                continue
            a, b = parts[q], parts[q + distance]
            parts[q] = jnp.where(upper, pltpu.roll(b, shift, 1), a)
            parts[q + distance] = jnp.where(upper, b, pltpu.roll(a, 128 - shift, 1))
        distance //= 2
    return parts


def dot(a, b):
    return jnp.dot(a, b, preferred_element_type=F32)


def iota(shape, axis):
    return lax.broadcasted_iota(I32, shape, axis)


def halves(x):
    high = x.astype(BF16)
    return high, (x - high.astype(F32)).astype(BF16)


def one_hot(mask):
    return jnp.where(mask, 1.0, 0.0).astype(BF16)


def looked_up(table, places):
    return jnp.take_along_axis(table, places, axis=1)


def permuted(table, order):
    upper, lower = order >> 7, order & 127
    out = jnp.zeros((ROWS, LANES), F32)
    for k in range(ROWS):
        line = jnp.broadcast_to(table[k : k + 1, :], (ROWS, LANES))
        out = jnp.where(upper == k, looked_up(line, lower), out)
    return out


def column(line):
    eye = iota((LANES, LANES), 0) == iota((LANES, LANES), 1)
    spread = jnp.where(eye, jnp.broadcast_to(line.astype(F32), (LANES, LANES)), 0.0)
    return dot(spread.astype(BF16), jnp.ones((LANES, LANES), BF16))


def block_sums(mats, start, vec):
    both = jnp.concatenate([vec, vec], axis=1)

    def step(n, total):
        cols = pl.ds(pl.multiple_of(256 * n, 256), 256)
        high, low = halves(mats[pl.ds(start, LANES), cols].astype(F32) * both)
        group = one_hot((iota((256, BLK), 0) >> 6) + 4 * n == iota((256, BLK), 1))
        return total + dot(jnp.concatenate([high, low], axis=0), group)

    total = lax.fori_loop(0, 16, step, jnp.zeros((256, BLK), F32))
    return total[:LANES] + total[LANES:]


def solve_kernel(
    charges, order, anchor, pairs, project_hbm, interp_hbm, near_hbm, k_hbm, fwd, bwd, into, back,
    out_ref,
    pv, iv, nv, ext, qd, codes, picks, zrow, slots, terms, field_ref, inverse,
    kv, halo_y, halo_x, halo_c, g0, s1, sb1, r1, sb2, r2, sb3, r3, sb4, r4, acc,
    fld, sy, sx, sc, ry, rx, rc, nb,
    in_sem, k_sem, hs_sem, hr_sem, ns_sem, nr_sem, s1_sem, r1_sem, s2_sem, r2_sem, s3_sem, r3_sem,
    s4_sem, r4_sem, os_sem, or_sem,
):
    row = lax.axis_index("row")
    col = lax.axis_index("col")
    mesh_id = pl.DeviceIdType.MESH

    def at(a, b):
        return (lax.rem(row + a + N, N), lax.rem(col + b + N, N))

    barrier = pltpu.get_barrier_semaphore()

    def greet(k, _):
        pl.semaphore_signal(barrier, inc=1, device_id=at(k, 0), device_id_type=mesh_id)
        pl.semaphore_signal(barrier, inc=1, device_id=at(0, k), device_id_type=mesh_id)
        return 0

    lax.fori_loop(1, N, greet, 0)
    for a in (-1, 1):
        for b in (-1, 1):
            pl.semaphore_signal(barrier, inc=1, device_id=at(a, b), device_id_type=mesh_id)
    p_copy = pltpu.make_async_copy(project_hbm, pv, in_sem.at[0])
    i_copy = pltpu.make_async_copy(interp_hbm, iv, in_sem.at[1])
    n_copy = pltpu.make_async_copy(near_hbm, nv, in_sem.at[2])
    p_copy.start()
    k_copies = [
        pltpu.make_async_copy(k_hbm.at[:, pl.ds(128 * h, 128)], kv.at[h], k_sem.at[h])
        for h in range(CH)
    ]
    for copy in k_copies:
        copy.start()
    n_copy.start()
    i_copy.start()

    permutation = order[...]
    q_slots = permuted(charges[...].astype(F32), permutation)
    block_of = iota((LANES, ROWS), 0) >> 1
    q_rows = dot(one_hot(block_of == iota((LANES, ROWS), 1)), q_slots.astype(BF16))
    odd = (iota((LANES, LANES), 0) & 1) == 1
    right = iota((LANES, LANES), 1) >= BLK
    q_both = jnp.where(odd == right, q_rows, pltpu.roll(q_rows, BLK, 1))
    qd[...] = q_both.astype(BF16)
    p_copy.wait()
    patch = block_sums(pv, 0, q_both)
    patch_high, patch_low = halves(patch)
    x0 = anchor[0:1, :] - 16 * row
    y0 = anchor[1:2, :] - 16 * col
    z0 = anchor[2:3, :]
    sheet = jnp.concatenate(
        [patch_high, patch_low] + [column(v).astype(BF16) for v in (z0, x0, y0)], axis=1
    )
    corner_rows = jnp.concatenate(
        [x0.astype(F32), y0.astype(F32), jnp.zeros((14, LANES), F32)], axis=0
    ).astype(BF16)
    ext[...] = jnp.zeros_like(ext)

    def code_of(x, y):
        inside = x * 16 + y
        past_y = 256 + (y - 16) * 16 + x
        past_x = 304 + (x - 16) * 16 + y
        corner = 352 + (x - 16) * 4 + (y - 16)
        return jnp.where(
            x < 16, jnp.where(y < 16, inside, past_y), jnp.where(y < 16, past_x, corner)
        )

    def scatter(n, _):
        rows = dot(one_hot((iota((256, LANES), 0) >> 4) + 16 * n == iota((256, LANES), 1)), sheet)
        point = iota((256, LANES), 0) & 15
        lane = iota((256, LANES), 1)
        z = rows[:, 128:256].astype(I32)
        x = rows[:, 256:384].astype(I32) + (point >> 2)
        y = rows[:, 384:512].astype(I32) + (point & 3)
        zrow[n] = z
        codes[n] = code_of(x, y)
        values = rows[:, 0:128] + pltpu.roll(rows[:, 0:128], BLK, 1)
        pieces = []
        for h in range(2):
            off = lane + 128 * h - z
            seen = (off >= 0) & (off < 4)
            places = 4 * point + jnp.clip(off, 0, 3)
            pieces += halves(jnp.where(seen, looked_up(values, places), 0.0))
        lines = dot(
            corner_rows,
            one_hot((iota((LANES, 256), 1) >> 4) + 16 * n == iota((LANES, 256), 0)),
        ).astype(I32)
        at_point = iota((1, 256), 1) & 15
        code = code_of(lines[0:1] + (at_point >> 2), lines[1:2] + (at_point & 3))
        pick = one_hot(iota((EXT, 256), 0) == code)
        added = dot(pick, jnp.concatenate(pieces, axis=1))
        ext[0] += added[:, 0:128] + added[:, 128:256]
        ext[1] += added[:, 256:384] + added[:, 384:512]
        return 0

    lax.fori_loop(0, 8, scatter, 0)
    pl.semaphore_wait(barrier, 2 * (N - 1) + 4)

    def remote(src, dst, send, recv, who):
        return pltpu.make_async_remote_copy(
            src_ref=src, dst_ref=dst, send_sem=send, recv_sem=recv,
            device_id=who, device_id_type=mesh_id,
        )

    def drained(ref, sem):
        pltpu.make_async_copy(ref, ref, sem).wait()

    halo_copies = [
        remote(ext.at[:, pl.ds(256, 48)], halo_y, hs_sem.at[0], hr_sem.at[0], at(0, 1)),
        remote(ext.at[:, pl.ds(304, 48)], halo_x, hs_sem.at[1], hr_sem.at[1], at(1, 0)),
        remote(ext.at[:, pl.ds(352, 16)], halo_c, hs_sem.at[2], hr_sem.at[2], at(1, 1)),
    ]
    for copy in halo_copies:
        copy.start()
    near_copies = []
    for k, (a, b) in enumerate(NEIGHBOURS):
        slot = NEIGHBOURS.index((-a, -b))
        near_copies.append(remote(qd, nb.at[slot], ns_sem.at[k], nr_sem.at[slot], at(a, b)))
    for copy in near_copies:
        copy.start()
    g0[...] = ext[:, :OWN, :]
    source = pairs[1:2, :]
    place = source >> 7
    slot = ((place >> 4) - row + 1) * 3 + ((place & 15) - col + 1)
    slot = jnp.where(slot == 4, 8, jnp.where(slot > 4, slot - 1, slot))
    for t in range(4):
        cut = slice(128 * t, 128 * t + 128)
        slots[t, 0:1] = slot[:, cut]
        slots[t, 1:2] = (source & 127)[:, cut]
    for copy in halo_copies:
        copy.wait()
    for h in range(2):
        for k in range(3):
            g0[h, pl.ds(k, 16, stride=16), :] += halo_y[h, 16 * k : 16 * k + 16, :]
        g0[h, 0:48, :] += halo_x[h]
        for k in range(3):
            g0[h, 16 * k : 16 * k + 4, :] += halo_c[h, 4 * k : 4 * k + 4, :]

    lanes = lax.broadcasted_iota(jnp.int32, (1, 128), 1)

    def exchange(src, dst, me, send, recv, along):
        def one(k, _):
            to = lax.rem(me + k, N)
            who = (row, to) if along == "col" else (to, col)
            remote(src.at[to], dst.at[me], send, recv, who).start()
            return 0

        lax.fori_loop(1, N, one, 0)
        dst[me] = src[me]

    grid = jnp.concatenate([g0[0], g0[1]], axis=1)
    high = grid.astype(BF16)
    low = (grid - high.astype(F32)).astype(BF16)
    s1[...] = (dot(high, fwd[0]) + dot(high, fwd[1]) + dot(low, fwd[0])).reshape(4, 4, 16, 512)
    for k in range(4):
        parts = [s1[:, q, :, 128 * k : 128 * k + 128].reshape(64, 128) for q in range(4)]
        for q, part in enumerate(transposed_groups(parts, lanes)):
            sb1[4 * k + q] = part.reshape(4, 16, 128).astype(BF16)
    exchange(sb1, r1, col, s1_sem, r1_sem, "col")
    drained(r1.at[pl.ds(0, N - 1)], r1_sem)

    def second(k, _):
        lines = dot(r1[:, 0].reshape(256, 128), into[k, 0:128])
        for j in range(1, 4):
            lines += dot(r1[:, j].reshape(256, 128), into[k, 128 * j : 128 * j + 128])
        lines = lines.astype(BF16)
        out = dot(bwd[0], lines) + dot(bwd[1], lines)
        sb2[k] = out.astype(BF16).reshape(N, 32, 128)
        exchange(sb2.at[k], r2.at[k], row, s2_sem.at[k], r2_sem.at[k], "row")
        return 0

    lax.fori_loop(0, CH, second, 0)
    for copy in k_copies:
        copy.wait()

    for copy in near_copies:
        copy.wait()
    n_copy.wait()

    def near_part(t):
        slot_rows = column(slots[t, 0:1]).astype(I32)
        place_rows = column(slots[t, 1:2]).astype(I32)
        lane = iota((LANES, LANES), 1)
        picked = jnp.zeros((LANES, LANES), F32)
        for s in range(9):
            table = qd[...] if s == 8 else nb[s]
            picked += dot(one_hot((slot_rows == s) & (place_rows == lane)), table)
        terms[t] = block_sums(nv, pl.multiple_of(128 * t, 128), picked)

    def first(k, _):
        near_part(k)
        drained(r2.at[k, pl.ds(0, N - 1)], r2_sem.at[k])
        halves = []
        for h in range(2):
            parts = [r2[k, 8 * h + q].astype(F32) for q in range(8)]
            halves.append(jnp.concatenate(transposed_groups(parts, lanes), axis=0).astype(BF16))
        lines = jnp.concatenate(halves, axis=1)
        spec = dot(lines, fwd[0]) + dot(lines, fwd[1])
        cols = []
        for h in range(CH):
            weights = jnp.concatenate(
                [kv[h, pl.ds(8 * k + q, 32, stride=32), :] for q in range(8)], axis=0
            )
            cols.append((spec[:, 128 * h : 128 * h + 128] * weights).astype(BF16))
        weighted = jnp.concatenate(cols, axis=1)
        field = dot(weighted, bwd[0]) + dot(weighted, bwd[1])
        for h in range(2):
            parts = [field[32 * q : 32 * q + 32, 128 * h : 128 * h + 128] for q in range(8)]
            for q, part in enumerate(transposed_groups(parts, lanes)):
                sb3[k, 8 * h + q] = part.astype(BF16)
        exchange(sb3.at[k], r3.at[k], row, s3_sem.at[k], r3_sem.at[k], "row")
        return 0

    lax.fori_loop(0, CH, first, 0)
    near = jnp.zeros((LANES, BLK), F32)
    for t in range(4):
        target = pairs[0:1, 128 * t : 128 * t + 128] - 128 * (row * N + col)
        hot = one_hot(iota((LANES, LANES), 0) == target)
        for part in halves(terms[t]):
            near += dot(hot, part)
    terms[0] = near
    inverse[...] = jnp.zeros_like(inverse)

    def inverted(k, total):
        lines = order[pl.ds(pl.multiple_of(8 * k, 8), 8), :]
        for j in range(8):
            line = lines[j : j + 1, :]
            at_row = iota((ROWS, LANES), 0) == (line >> 7)
            both = jnp.concatenate(
                [
                    jnp.where(at_row, iota((ROWS, LANES), 1).astype(F32), 0.0),
                    jnp.where(at_row, (8 * k + j).astype(F32), 0.0),
                ],
                axis=0,
            ).astype(BF16)
            hot = one_hot(iota((LANES, LANES), 0) == (line & 127))
            total += lax.dot_general(
                both, hot, (((1,), (1,)), ((), ())), preferred_element_type=F32
            )
        return total

    def picking(n):
        for j in range(3):
            lane = iota((256, LANES), 1) + 128 * j
            picks[n, :, 128 * j : 128 * j + 128] = one_hot(codes[n] == lane)

    acc[...] = jnp.zeros_like(acc)

    def second_back(k, _):
        inverse[...] += inverted(2 * k, inverted(2 * k + 1, jnp.zeros((LANES, LANES), F32)))
        picking(2 * k)
        picking(2 * k + 1)
        drained(r3.at[k, pl.ds(0, N - 1)], r3_sem.at[k])
        lines = r3[k].reshape(512, 128)
        part = (dot(fwd[0], lines) + dot(fwd[1], lines)).astype(BF16)
        acc[...] += dot(part, back[k])
        return 0

    lax.fori_loop(0, CH, second_back, 0)
    for j in range(4):
        sb4[:, j] = acc[:, 128 * j : 128 * j + 128].astype(BF16).reshape(16, 16, 128)
    exchange(sb4, r4, col, s4_sem, r4_sem, "col")
    drained(r4.at[pl.ds(0, N - 1)], r4_sem)
    for k in range(4):
        parts = [r4[4 * k + q].astype(F32).reshape(64, 128) for q in range(4)]
        for q, part in enumerate(transposed_groups(parts, lanes)):
            s1[:, q, :, 128 * k : 128 * k + 128] = part.reshape(4, 16, 128)
    lines = s1[...].reshape(256, 512).astype(BF16)
    field = dot(lines, bwd[0]) + dot(lines, bwd[1])
    for h in range(2):
        fld[h] = field[:, 128 * h : 128 * h + 128]
    sx[...] = field[0:48].astype(BF16)
    for h in range(2):
        sy[:, 128 * h : 128 * h + 128] = jnp.concatenate(
            [fld[h, pl.ds(k, 16, stride=16), :] for k in range(3)], axis=0
        ).astype(BF16)
        sc[:, 128 * h : 128 * h + 128] = jnp.concatenate(
            [fld[h, 16 * k : 16 * k + 4, :] for k in range(4)], axis=0
        ).astype(BF16)
    out_copies = [
        remote(sy, ry, os_sem.at[0], or_sem.at[0], at(0, -1)),
        remote(sx, rx, os_sem.at[1], or_sem.at[1], at(-1, 0)),
        remote(sc, rc, os_sem.at[2], or_sem.at[2], at(-1, -1)),
    ]
    for copy in out_copies:
        copy.start()
    field_ref[0:OWN] = field.astype(BF16)
    field_ref[EXT:PICK] = jnp.zeros((PICK - EXT, G), BF16)
    drained(sb1.at[pl.ds(0, N - 1)], s1_sem)
    drained(sb4.at[pl.ds(0, N - 1)], s4_sem)
    for k in range(CH):
        drained(sb2.at[k, pl.ds(0, N - 1)], s2_sem.at[k])
        drained(sb3.at[k, pl.ds(0, N - 1)], s3_sem.at[k])
    for copy in out_copies:
        copy.wait()
    field_ref[256:304] = ry[...]
    field_ref[304:352] = rx[...]
    field_ref[352:368] = rc[...]
    i_copy.wait()

    def gathered(n, _):
        taken = dot(picks[n], field_ref[...])
        point = iota((256, LANES), 0) & 15
        lane = iota((256, LANES), 1)
        z = zrow[n] + (lane & 3)
        value = jnp.where(
            z < 128,
            looked_up(taken[:, 0:128], jnp.minimum(z, 127)),
            looked_up(taken[:, 128:256], jnp.maximum(z - 128, 0)),
        )
        value = jnp.where(((lane >> 2) & 15) == point, value, 0.0)
        fld[0, pl.ds(pl.multiple_of(16 * n, 16), 16), :] = jnp.sum(
            value.reshape(16, 16, LANES), axis=1
        )
        return 0

    lax.fori_loop(0, 8, gathered, 0)
    total = block_sums(iv, 0, fld[0, 0:LANES, :]) + terms[0]
    total = jnp.concatenate([total, total], axis=1)
    total = jnp.where(odd == right, total, 0.0)
    gather_rows = one_hot(iota((ROWS, LANES), 0) == (iota((ROWS, LANES), 1) >> 1))
    by_slot = sum(dot(gather_rows, part) for part in halves(total))
    back_order = inverse[...].astype(I32)
    out_ref[...] = permuted(by_slot, back_order[ROWS:] * 128 + back_order[:ROWS])


def solve(charges, order, anchor, pairs, project, interpolate, near_blocks, kernel_spectrum):
    forward, backward, into, back = tables()
    vmem = pl.BlockSpec(memory_space=pltpu.VMEM)
    hbm = pl.BlockSpec(memory_space=pl.ANY)
    dma = pltpu.SemaphoreType.DMA
    return pl.pallas_call(
        solve_kernel,
        out_shape=jax.ShapeDtypeStruct((ROWS, LANES), F32),
        in_specs=[vmem] * 4 + [hbm] * 4 + [vmem] * 4,
        out_specs=vmem,
        scratch_shapes=[
            pltpu.VMEM((128, 4096), BF16),
            pltpu.VMEM((128, 4096), BF16),
            pltpu.VMEM((512, 4096), BF16),
            pltpu.VMEM((2, EXT, 128), F32),
            pltpu.VMEM((LANES, LANES), BF16),
            pltpu.VMEM((8, 256, LANES), I32),
            pltpu.VMEM((8, 256, PICK), BF16),
            pltpu.VMEM((8, 256, LANES), I32),
            pltpu.VMEM((4, 8, LANES), I32),
            pltpu.VMEM((4, LANES, BLK), F32),
            pltpu.VMEM((PICK, G), BF16),
            pltpu.VMEM((LANES, LANES), F32),
            pltpu.VMEM((CH, 1024, 128), F32),
            pltpu.VMEM((2, 48, 128), F32),
            pltpu.VMEM((2, 48, 128), F32),
            pltpu.VMEM((2, 16, 128), F32),
            pltpu.VMEM((2, OWN, 128), F32),
            pltpu.VMEM((4, 4, 16, 512), F32),
            pltpu.VMEM((N, 4, 16, 128), BF16),
            pltpu.VMEM((N, 4, 16, 128), BF16),
            pltpu.VMEM((CH, N, 32, 128), BF16),
            pltpu.VMEM((CH, N, 32, 128), BF16),
            pltpu.VMEM((CH, N, 32, 128), BF16),
            pltpu.VMEM((CH, N, 32, 128), BF16),
            pltpu.VMEM((N, 4, 16, 128), BF16),
            pltpu.VMEM((N, 4, 16, 128), BF16),
            pltpu.VMEM((OWN, P_SIZE), F32),
            pltpu.VMEM((2, OWN, 128), F32),
            pltpu.VMEM((48, G), BF16),
            pltpu.VMEM((48, G), BF16),
            pltpu.VMEM((16, G), BF16),
            pltpu.VMEM((48, G), BF16),
            pltpu.VMEM((48, G), BF16),
            pltpu.VMEM((16, G), BF16),
            pltpu.VMEM((8, LANES, LANES), BF16),
            dma((3,)),
            dma((CH,)),
            dma((3,)),
            dma((3,)),
            dma((8,)),
            dma((8,)),
            dma(()),
            dma(()),
            dma((CH,)),
            dma((CH,)),
            dma((CH,)),
            dma((CH,)),
            dma(()),
            dma(()),
            dma((3,)),
            dma((3,)),
        ],
        compiler_params=pltpu.CompilerParams(
            collective_id=0, has_side_effects=True, vmem_limit_bytes=48 << 20
        ),
    )(
        charges.reshape(ROWS, LANES),
        order.reshape(ROWS, LANES),
        anchor,
        pairs,
        project,
        interpolate,
        near_blocks,
        kernel_spectrum.reshape(1024, P_SIZE),
        jnp.asarray(forward),
        jnp.asarray(backward),
        jnp.asarray(into),
        jnp.asarray(back),
    )


def body(
    charges,
    panel_order,
    patch_anchor,
    project,
    interpolate,
    kernel_spectrum,
    near_pairs,
    near_blocks,
):
    out = solve(
        charges, panel_order, patch_anchor, near_pairs, project, interpolate, near_blocks,
        kernel_spectrum,
    )
    return out.reshape(ROWS * LANES)


def solution(mesh):
    placed = (
        P(("row", "col")),
        P(("row", "col")),
        P(None, ("row", "col")),
        P(("row", "col"), None),
        P(("row", "col"), None),
        P("row", "col", None),
        P(None, ("row", "col")),
        P(("row", "col"), None),
    )
    return jax.shard_map(
        body, mesh=mesh, in_specs=placed, out_specs=P(("row", "col")), check_vma=False
    )
```

```python
import math

import jax
import jax.numpy as jnp
import numpy as np
from jax import lax
from jax.experimental import pallas as pl
from jax.experimental.pallas import tpu as pltpu
from jax.sharding import PartitionSpec as P

G = 256
P_SIZE = 512
BLK = 64
PTS = 64
N = 16
OWN = 256
EXT = 368
CH = 4
F32 = jnp.float32
BF16 = jnp.bfloat16
LANES = 128
ROWS = 64
PICK = 384
I32 = jnp.int32
NEIGHBOURS = [(a, b) for a in (-1, 0, 1) for b in (-1, 0, 1) if (a, b) != (0, 0)]


def tables():
    first = np.arange(G)[:, None]
    second = np.arange(P_SIZE)[None, :]
    phase = (first * second % P_SIZE).astype(np.float64) * (2.0 * math.pi / P_SIZE)
    table = (np.cos(phase) + np.sin(phase)) / math.sqrt(P_SIZE)
    high = table.astype(BF16)
    low = (table - high.astype(np.float64)).astype(BF16)
    forward = np.stack([high, low])
    backward = np.stack([high.T, low.T])
    swap = np.zeros((P_SIZE, P_SIZE), np.float32)
    x, f = np.meshgrid(np.arange(16), np.arange(32), indexing="ij")
    swap[x * 32 + f, f * 16 + x] = 1.0
    swap = swap.astype(BF16)
    into = np.stack([swap[:, 128 * k : 128 * k + 128] for k in range(CH)])
    back = np.stack([swap.T[128 * k : 128 * k + 128, :] for k in range(CH)])
    return forward, backward, into, back


def transposed_groups(parts, lanes):
    count = len(parts)
    group = 128 // count
    distance = count // 2
    parts = list(parts)
    while distance:
        shift = distance * group
        upper = (lanes // shift) % 2 == 1
        for q in range(count):
            if q & distance:
                continue
            a, b = parts[q], parts[q + distance]
            parts[q] = jnp.where(upper, pltpu.roll(b, shift, 1), a)
            parts[q + distance] = jnp.where(upper, b, pltpu.roll(a, 128 - shift, 1))
        distance //= 2
    return parts


def dot(a, b):
    return jnp.dot(a, b, preferred_element_type=F32)


def iota(shape, axis):
    return lax.broadcasted_iota(I32, shape, axis)


def halves(x):
    high = x.astype(BF16)
    return high, (x - high.astype(F32)).astype(BF16)


def one_hot(mask):
    return jnp.where(mask, 1.0, 0.0).astype(BF16)


def looked_up(table, places):
    return jnp.take_along_axis(table, places, axis=1)


def permuted(table, order):
    upper, lower = order >> 7, order & 127
    out = jnp.zeros((ROWS, LANES), F32)
    for k in range(ROWS):
        line = jnp.broadcast_to(table[k : k + 1, :], (ROWS, LANES))
        out = jnp.where(upper == k, looked_up(line, lower), out)
    return out


def column(line):
    eye = iota((LANES, LANES), 0) == iota((LANES, LANES), 1)
    spread = jnp.where(eye, jnp.broadcast_to(line.astype(F32), (LANES, LANES)), 0.0)
    return dot(spread.astype(BF16), jnp.ones((LANES, LANES), BF16))


def block_sums(mats, start, vec, group):
    high, low = [], []
    for n in range(32):
        part = mats[pl.ds(start, LANES), 128 * n : 128 * n + 128].astype(F32) * vec
        one, two = halves(part)
        high.append(one)
        low.append(two)
    total = jnp.zeros((256, LANES), F32)
    for q in range(4):
        cut = slice(8 * q, 8 * q + 8)
        both = jnp.concatenate(
            [jnp.concatenate(high[cut], axis=1), jnp.concatenate(low[cut], axis=1)], axis=0
        )
        total += dot(both, group[1024 * q : 1024 * q + 1024])
    return total[:LANES] + total[LANES:]


def solve_kernel(
    charges_hbm, order_hbm, anchor_hbm, pairs_hbm, project_hbm, interp_hbm, near_hbm, k_hbm,
    fwd_hbm, bwd_hbm, into_hbm, back_hbm,
    out_ref,
    charges, order, anchor, pairs, fwd, bwd, into, back, group, spots, placed, pick,
    pv, iv, nv, ext, qd, codes, picks, zrow, slots, terms, field_ref, inverse,
    kv, halo_y, halo_x, halo_c, g0, s1, sb1, r1, sb2, r2, sb3, r3, sb4, r4, acc,
    fld, sy, sx, sc, ry, rx, rc, nb,
    in_sem, k_sem, hs_sem, hr_sem, ns_sem, nr_sem, s1_sem, r1_sem, s2_sem, r2_sem, s3_sem, r3_sem,
    s4_sem, r4_sem, os_sem, or_sem,
):
    row = lax.axis_index("row")
    col = lax.axis_index("col")
    mesh_id = pl.DeviceIdType.MESH

    def at(a, b):
        return (lax.rem(row + a + N, N), lax.rem(col + b + N, N))

    barrier = pltpu.get_barrier_semaphore()

    def greet(k, _):
        pl.semaphore_signal(barrier, inc=1, device_id=at(k, 0), device_id_type=mesh_id)
        pl.semaphore_signal(barrier, inc=1, device_id=at(0, k), device_id_type=mesh_id)
        return 0

    lax.fori_loop(1, N, greet, 0)
    for a in (-1, 1):
        for b in (-1, 1):
            pl.semaphore_signal(barrier, inc=1, device_id=at(a, b), device_id_type=mesh_id)
    small = [
        pltpu.make_async_copy(src, dst, in_sem.at[3 + n])
        for n, (src, dst) in enumerate(
            [
                (order_hbm, order), (charges_hbm, charges), (anchor_hbm, anchor),
                (pairs_hbm, pairs), (fwd_hbm, fwd), (bwd_hbm, bwd), (into_hbm, into),
                (back_hbm, back),
            ]
        )
    ]
    for copy in small[:4]:
        copy.start()
    p_copy = pltpu.make_async_copy(project_hbm, pv, in_sem.at[0])
    i_copy = pltpu.make_async_copy(interp_hbm, iv, in_sem.at[1])
    n_copy = pltpu.make_async_copy(near_hbm, nv, in_sem.at[2])
    p_copy.start()
    for copy in small[4:]:
        copy.start()
    k_copies = [
        pltpu.make_async_copy(k_hbm.at[:, pl.ds(128 * h, 128)], kv.at[h], k_sem.at[h])
        for h in range(CH)
    ]
    for copy in k_copies:
        copy.start()
    n_copy.start()
    i_copy.start()

    def grouped(n, _):
        rows = pl.ds(pl.multiple_of(512 * n, 512), 512)
        group[rows] = one_hot(
            (iota((512, LANES), 0) >> 6) + 8 * n == (iota((512, LANES), 1) & (BLK - 1))
        )
        return 0

    lax.fori_loop(0, 8, grouped, 0)
    for copy in small[:4]:
        copy.wait()
    permutation = order[...]
    q_slots = permuted(charges[...].astype(F32), permutation)
    block_of = iota((LANES, ROWS), 0) >> 1
    q_rows = dot(one_hot(block_of == iota((LANES, ROWS), 1)), q_slots.astype(BF16))
    odd = (iota((LANES, LANES), 0) & 1) == 1
    right = iota((LANES, LANES), 1) >= BLK
    q_both = jnp.where(odd == right, q_rows, pltpu.roll(q_rows, BLK, 1))
    qd[...] = q_both.astype(BF16)
    p_copy.wait()
    patch = block_sums(pv, 0, q_both, group)
    patch_high, patch_low = halves(patch[:, :BLK])
    x0 = anchor[0:1, :] - 16 * row
    y0 = anchor[1:2, :] - 16 * col
    z0 = anchor[2:3, :]
    sheet = jnp.concatenate(
        [patch_high, patch_low] + [column(v).astype(BF16) for v in (z0, x0, y0)], axis=1
    )
    corner_rows = jnp.concatenate(
        [x0.astype(F32), y0.astype(F32), jnp.zeros((14, LANES), F32)], axis=0
    ).astype(BF16)
    def code_of(x, y):
        inside = x * 16 + y
        past_y = 256 + (y - 16) * 16 + x
        past_x = 304 + (x - 16) * 16 + y
        corner = 352 + (x - 16) * 4 + (y - 16)
        return jnp.where(
            x < 16, jnp.where(y < 16, inside, past_y), jnp.where(y < 16, past_x, corner)
        )

    lines = dot(
        corner_rows, one_hot((iota((LANES, 2048), 1) >> 4) == iota((LANES, 2048), 0))
    ).astype(I32)
    at_point = iota((1, 2048), 1) & 15
    spots[0:1] = code_of(lines[0:1] + (at_point >> 2), lines[1:2] + (at_point & 3))

    def scatter(n, _):
        rows = dot(one_hot((iota((256, LANES), 0) >> 4) + 16 * n == iota((256, LANES), 1)), sheet)
        point = iota((256, LANES), 0) & 15
        lane = iota((256, LANES), 1)
        z = rows[:, 128:256].astype(I32)
        x = rows[:, 256:384].astype(I32) + (point >> 2)
        y = rows[:, 384:512].astype(I32) + (point & 3)
        zrow[n] = z
        codes[n] = code_of(x, y)
        values = rows[:, 0:128] + pltpu.roll(rows[:, 0:128], BLK, 1)
        pieces = []
        for h in range(2):
            off = lane + 128 * h - z
            seen = (off >= 0) & (off < 4)
            places = 4 * point + jnp.clip(off, 0, 3)
            pieces += halves(jnp.where(seen, looked_up(values, places), 0.0))
        here = pl.ds(pl.multiple_of(256 * n, 256), 256)
        placed[here] = jnp.concatenate(pieces, axis=1)
        pick[:, here] = one_hot(iota((EXT, 256), 0) == spots[0:1, here])
        return 0

    lax.fori_loop(0, 8, scatter, 0, unroll=2)
    added = dot(pick[...], placed[...])
    ext[0] = added[:, 0:128] + added[:, 128:256]
    ext[1] = added[:, 256:384] + added[:, 384:512]
    for copy in small[4:]:
        copy.wait()
    pl.semaphore_wait(barrier, 2 * (N - 1) + 4)

    def remote(src, dst, send, recv, who):
        return pltpu.make_async_remote_copy(
            src_ref=src, dst_ref=dst, send_sem=send, recv_sem=recv,
            device_id=who, device_id_type=mesh_id,
        )

    def drained(ref, sem):
        pltpu.make_async_copy(ref, ref, sem).wait()

    halo_copies = [
        remote(ext.at[:, pl.ds(256, 48)], halo_y, hs_sem.at[0], hr_sem.at[0], at(0, 1)),
        remote(ext.at[:, pl.ds(304, 48)], halo_x, hs_sem.at[1], hr_sem.at[1], at(1, 0)),
        remote(ext.at[:, pl.ds(352, 16)], halo_c, hs_sem.at[2], hr_sem.at[2], at(1, 1)),
    ]
    for copy in halo_copies:
        copy.start()
    near_copies = []
    for k, (a, b) in enumerate(NEIGHBOURS):
        slot = NEIGHBOURS.index((-a, -b))
        near_copies.append(remote(qd, nb.at[slot], ns_sem.at[k], nr_sem.at[slot], at(a, b)))
    for copy in near_copies:
        copy.start()
    g0[...] = ext[:, :OWN, :]
    source = pairs[1:2, :]
    place = source >> 7
    slot = ((place >> 4) - row + 1) * 3 + ((place & 15) - col + 1)
    slot = jnp.where(slot == 4, 8, jnp.where(slot > 4, slot - 1, slot))
    for t in range(4):
        cut = slice(128 * t, 128 * t + 128)
        slots[t, 0:1] = slot[:, cut]
        slots[t, 1:2] = (source & 127)[:, cut]
    for copy in halo_copies:
        copy.wait()
    for h in range(2):
        for k in range(3):
            g0[h, pl.ds(k, 16, stride=16), :] += halo_y[h, 16 * k : 16 * k + 16, :]
        g0[h, 0:48, :] += halo_x[h]
        for k in range(3):
            g0[h, 16 * k : 16 * k + 4, :] += halo_c[h, 4 * k : 4 * k + 4, :]

    lanes = lax.broadcasted_iota(jnp.int32, (1, 128), 1)

    def exchange(src, dst, me, send, recv, along):
        def one(k, _):
            to = lax.rem(me + k, N)
            who = (row, to) if along == "col" else (to, col)
            remote(src.at[to], dst.at[me], send, recv, who).start()
            return 0

        lax.fori_loop(1, N, one, 0)
        dst[me] = src[me]

    grid = jnp.concatenate([g0[0], g0[1]], axis=1)
    high = grid.astype(BF16)
    low = (grid - high.astype(F32)).astype(BF16)
    s1[...] = (dot(high, fwd[0]) + dot(high, fwd[1]) + dot(low, fwd[0])).reshape(4, 4, 16, 512)
    for k in range(4):
        parts = [s1[:, q, :, 128 * k : 128 * k + 128].reshape(64, 128) for q in range(4)]
        for q, part in enumerate(transposed_groups(parts, lanes)):
            sb1[4 * k + q] = part.reshape(4, 16, 128).astype(BF16)
    exchange(sb1, r1, col, s1_sem, r1_sem, "col")
    drained(r1.at[pl.ds(0, N - 1)], r1_sem)

    def second(k, _):
        lines = dot(r1[:, 0].reshape(256, 128), into[k, 0:128])
        for j in range(1, 4):
            lines += dot(r1[:, j].reshape(256, 128), into[k, 128 * j : 128 * j + 128])
        lines = lines.astype(BF16)
        out = dot(bwd[0], lines) + dot(bwd[1], lines)
        sb2[k] = out.astype(BF16).reshape(N, 32, 128)
        exchange(sb2.at[k], r2.at[k], row, s2_sem.at[k], r2_sem.at[k], "row")
        return 0

    lax.fori_loop(0, CH, second, 0)
    for copy in k_copies:
        copy.wait()

    for copy in near_copies:
        copy.wait()
    n_copy.wait()

    def near_part(t):
        slot_rows = column(slots[t, 0:1]).astype(I32)
        place_rows = column(slots[t, 1:2]).astype(I32)
        lane = iota((LANES, LANES), 1)
        picked = jnp.zeros((LANES, LANES), F32)
        for s in range(9):
            table = qd[...] if s == 8 else nb[s]
            picked += dot(one_hot((slot_rows == s) & (place_rows == lane)), table)
        terms[t] = block_sums(nv, pl.multiple_of(128 * t, 128), picked, group)

    def first(k, _):
        near_part(k)
        drained(r2.at[k, pl.ds(0, N - 1)], r2_sem.at[k])
        halves = []
        for h in range(2):
            parts = [r2[k, 8 * h + q].astype(F32) for q in range(8)]
            halves.append(jnp.concatenate(transposed_groups(parts, lanes), axis=0).astype(BF16))
        lines = jnp.concatenate(halves, axis=1)
        spec = dot(lines, fwd[0]) + dot(lines, fwd[1])
        cols = []
        for h in range(CH):
            weights = jnp.concatenate(
                [kv[h, pl.ds(8 * k + q, 32, stride=32), :] for q in range(8)], axis=0
            )
            cols.append((spec[:, 128 * h : 128 * h + 128] * weights).astype(BF16))
        weighted = jnp.concatenate(cols, axis=1)
        field = dot(weighted, bwd[0]) + dot(weighted, bwd[1])
        for h in range(2):
            parts = [field[32 * q : 32 * q + 32, 128 * h : 128 * h + 128] for q in range(8)]
            for q, part in enumerate(transposed_groups(parts, lanes)):
                sb3[k, 8 * h + q] = part.astype(BF16)
        exchange(sb3.at[k], r3.at[k], row, s3_sem.at[k], r3_sem.at[k], "row")
        return 0

    lax.fori_loop(0, CH, first, 0)
    near = jnp.zeros((LANES, LANES), F32)
    for t in range(4):
        target = pairs[0:1, 128 * t : 128 * t + 128] - 128 * (row * N + col)
        hot = one_hot(iota((LANES, LANES), 0) == target)
        for part in halves(terms[t]):
            near += dot(hot, part)
    terms[0] = near
    inverse[...] = jnp.zeros_like(inverse)

    def inverted(k, total):
        lines = order[pl.ds(pl.multiple_of(8 * k, 8), 8), :]
        for j in range(8):
            line = lines[j : j + 1, :]
            at_row = iota((ROWS, LANES), 0) == (line >> 7)
            both = jnp.concatenate(
                [
                    jnp.where(at_row, iota((ROWS, LANES), 1).astype(F32), 0.0),
                    jnp.where(at_row, (8 * k + j).astype(F32), 0.0),
                ],
                axis=0,
            ).astype(BF16)
            hot = one_hot(iota((LANES, LANES), 0) == (line & 127))
            total += lax.dot_general(
                both, hot, (((1,), (1,)), ((), ())), preferred_element_type=F32
            )
        return total

    def picking(n):
        for j in range(3):
            lane = iota((256, LANES), 1) + 128 * j
            picks[n, :, 128 * j : 128 * j + 128] = one_hot(codes[n] == lane)

    acc[...] = jnp.zeros_like(acc)

    def second_back(k, _):
        inverse[...] += inverted(2 * k, inverted(2 * k + 1, jnp.zeros((LANES, LANES), F32)))
        picking(2 * k)
        picking(2 * k + 1)
        drained(r3.at[k, pl.ds(0, N - 1)], r3_sem.at[k])
        lines = r3[k].reshape(512, 128)
        part = (dot(fwd[0], lines) + dot(fwd[1], lines)).astype(BF16)
        acc[...] += dot(part, back[k])
        return 0

    lax.fori_loop(0, CH, second_back, 0)
    for j in range(4):
        sb4[:, j] = acc[:, 128 * j : 128 * j + 128].astype(BF16).reshape(16, 16, 128)
    exchange(sb4, r4, col, s4_sem, r4_sem, "col")
    drained(r4.at[pl.ds(0, N - 1)], r4_sem)
    for k in range(4):
        parts = [r4[4 * k + q].astype(F32).reshape(64, 128) for q in range(4)]
        for q, part in enumerate(transposed_groups(parts, lanes)):
            s1[:, q, :, 128 * k : 128 * k + 128] = part.reshape(4, 16, 128)
    lines = s1[...].reshape(256, 512).astype(BF16)
    field = dot(lines, bwd[0]) + dot(lines, bwd[1])
    for h in range(2):
        fld[h] = field[:, 128 * h : 128 * h + 128]
    sx[...] = field[0:48].astype(BF16)
    for h in range(2):
        sy[:, 128 * h : 128 * h + 128] = jnp.concatenate(
            [fld[h, pl.ds(k, 16, stride=16), :] for k in range(3)], axis=0
        ).astype(BF16)
        sc[:, 128 * h : 128 * h + 128] = jnp.concatenate(
            [fld[h, 16 * k : 16 * k + 4, :] for k in range(4)], axis=0
        ).astype(BF16)
    out_copies = [
        remote(sy, ry, os_sem.at[0], or_sem.at[0], at(0, -1)),
        remote(sx, rx, os_sem.at[1], or_sem.at[1], at(-1, 0)),
        remote(sc, rc, os_sem.at[2], or_sem.at[2], at(-1, -1)),
    ]
    for copy in out_copies:
        copy.start()
    field_ref[0:OWN] = field.astype(BF16)
    field_ref[EXT:PICK] = jnp.zeros((PICK - EXT, G), BF16)
    drained(sb1.at[pl.ds(0, N - 1)], s1_sem)
    drained(sb4.at[pl.ds(0, N - 1)], s4_sem)
    for k in range(CH):
        drained(sb2.at[k, pl.ds(0, N - 1)], s2_sem.at[k])
        drained(sb3.at[k, pl.ds(0, N - 1)], s3_sem.at[k])
    for copy in out_copies:
        copy.wait()
    field_ref[256:304] = ry[...]
    field_ref[304:352] = rx[...]
    field_ref[352:368] = rc[...]
    i_copy.wait()

    def gathered(n, _):
        taken = dot(picks[n], field_ref[...])
        point = iota((256, LANES), 0) & 15
        lane = iota((256, LANES), 1)
        z = zrow[n] + (lane & 3)
        value = jnp.where(
            z < 128,
            looked_up(taken[:, 0:128], jnp.minimum(z, 127)),
            looked_up(taken[:, 128:256], jnp.maximum(z - 128, 0)),
        )
        value = jnp.where(((lane >> 2) & 15) == point, value, 0.0)
        fld[0, pl.ds(pl.multiple_of(16 * n, 16), 16), :] = jnp.sum(
            value.reshape(16, 16, LANES), axis=1
        )
        return 0

    lax.fori_loop(0, 8, gathered, 0, unroll=2)
    total = block_sums(iv, 0, fld[0, 0:LANES, :], group) + terms[0]
    total = jnp.where(odd == right, total, 0.0)
    gather_rows = one_hot(iota((ROWS, LANES), 0) == (iota((ROWS, LANES), 1) >> 1))
    by_slot = sum(dot(gather_rows, part) for part in halves(total))
    back_order = inverse[...].astype(I32)
    out_ref[...] = permuted(by_slot, back_order[ROWS:] * 128 + back_order[:ROWS])


def solve(charges, order, anchor, pairs, project, interpolate, near_blocks, kernel_spectrum):
    forward, backward, into, back = tables()
    vmem = pl.BlockSpec(memory_space=pltpu.VMEM)
    hbm = pl.BlockSpec(memory_space=pl.ANY)
    dma = pltpu.SemaphoreType.DMA
    return pl.pallas_call(
        solve_kernel,
        out_shape=jax.ShapeDtypeStruct((ROWS, LANES), F32),
        in_specs=[hbm] * 12,
        out_specs=vmem,
        scratch_shapes=[
            pltpu.VMEM((ROWS, LANES), BF16),
            pltpu.VMEM((ROWS, LANES), I32),
            pltpu.VMEM((3, LANES), I32),
            pltpu.VMEM((2, 512), I32),
            pltpu.VMEM((2, 256, 512), BF16),
            pltpu.VMEM((2, 512, 256), BF16),
            pltpu.VMEM((4, 512, 128), BF16),
            pltpu.VMEM((4, 128, 512), BF16),
            pltpu.VMEM((4096, LANES), BF16),
            pltpu.VMEM((8, 2048), I32),
            pltpu.VMEM((2048, 512), BF16),
            pltpu.VMEM((EXT, 2048), BF16),
            pltpu.VMEM((128, 4096), BF16),
            pltpu.VMEM((128, 4096), BF16),
            pltpu.VMEM((512, 4096), BF16),
            pltpu.VMEM((2, EXT, 128), F32),
            pltpu.VMEM((LANES, LANES), BF16),
            pltpu.VMEM((8, 256, LANES), I32),
            pltpu.VMEM((8, 256, PICK), BF16),
            pltpu.VMEM((8, 256, LANES), I32),
            pltpu.VMEM((4, 8, LANES), I32),
            pltpu.VMEM((4, LANES, LANES), F32),
            pltpu.VMEM((PICK, G), BF16),
            pltpu.VMEM((LANES, LANES), F32),
            pltpu.VMEM((CH, 1024, 128), F32),
            pltpu.VMEM((2, 48, 128), F32),
            pltpu.VMEM((2, 48, 128), F32),
            pltpu.VMEM((2, 16, 128), F32),
            pltpu.VMEM((2, OWN, 128), F32),
            pltpu.VMEM((4, 4, 16, 512), F32),
            pltpu.VMEM((N, 4, 16, 128), BF16),
            pltpu.VMEM((N, 4, 16, 128), BF16),
            pltpu.VMEM((CH, N, 32, 128), BF16),
            pltpu.VMEM((CH, N, 32, 128), BF16),
            pltpu.VMEM((CH, N, 32, 128), BF16),
            pltpu.VMEM((CH, N, 32, 128), BF16),
            pltpu.VMEM((N, 4, 16, 128), BF16),
            pltpu.VMEM((N, 4, 16, 128), BF16),
            pltpu.VMEM((OWN, P_SIZE), F32),
            pltpu.VMEM((2, OWN, 128), F32),
            pltpu.VMEM((48, G), BF16),
            pltpu.VMEM((48, G), BF16),
            pltpu.VMEM((16, G), BF16),
            pltpu.VMEM((48, G), BF16),
            pltpu.VMEM((48, G), BF16),
            pltpu.VMEM((16, G), BF16),
            pltpu.VMEM((8, LANES, LANES), BF16),
            dma((11,)),
            dma((CH,)),
            dma((3,)),
            dma((3,)),
            dma((8,)),
            dma((8,)),
            dma(()),
            dma(()),
            dma((CH,)),
            dma((CH,)),
            dma((CH,)),
            dma((CH,)),
            dma(()),
            dma(()),
            dma((3,)),
            dma((3,)),
        ],
        compiler_params=pltpu.CompilerParams(
            collective_id=0, has_side_effects=True, vmem_limit_bytes=62 << 20
        ),
    )(
        charges.reshape(ROWS, LANES),
        order.reshape(ROWS, LANES),
        anchor,
        pairs,
        project,
        interpolate,
        near_blocks,
        kernel_spectrum.reshape(1024, P_SIZE),
        jnp.asarray(forward),
        jnp.asarray(backward),
        jnp.asarray(into),
        jnp.asarray(back),
    )


def body(
    charges,
    panel_order,
    patch_anchor,
    project,
    interpolate,
    kernel_spectrum,
    near_pairs,
    near_blocks,
):
    out = solve(
        charges, panel_order, patch_anchor, near_pairs, project, interpolate, near_blocks,
        kernel_spectrum,
    )
    return out.reshape(ROWS * LANES)


def solution(mesh):
    placed = (
        P(("row", "col")),
        P(("row", "col")),
        P(None, ("row", "col")),
        P(("row", "col"), None),
        P(("row", "col"), None),
        P("row", "col", None),
        P(None, ("row", "col")),
        P(("row", "col"), None),
    )
    return jax.shard_map(
        body, mesh=mesh, in_specs=placed, out_specs=P(("row", "col")), check_vma=False
    )
```

```python
import math

import jax
import jax.numpy as jnp
import numpy as np
from jax import lax
from jax.experimental import pallas as pl
from jax.experimental.pallas import tpu as pltpu
from jax.sharding import PartitionSpec as P

G = 256
P_SIZE = 512
BLK = 64
PTS = 64
N = 16
TALL = 24
WIDE = 20
EXT = TALL * WIDE
CH = 2
F32 = jnp.float32
BF16 = jnp.bfloat16
LANES = 128
ROWS = 64
PICK = 512
I32 = jnp.int32
NEIGHBOURS = [(a, b) for a in (-1, 0, 1) for b in (-1, 0, 1) if (a, b) != (0, 0)]


def tables():
    first = np.arange(G)[:, None]
    second = np.arange(P_SIZE)[None, :]
    phase = (first * second % P_SIZE).astype(np.float64) * (2.0 * math.pi / P_SIZE)
    table = (np.cos(phase) + np.sin(phase)) / math.sqrt(P_SIZE)
    high = table.astype(BF16)
    low = (table - high.astype(np.float64)).astype(BF16)
    backward = np.stack([high.T, low.T])
    reach = np.zeros((N, TALL), np.int64) - 1
    for c in range(N):
        for y in range(19):
            if 16 * c + y < G:
                reach[c, y] = 16 * c + y
    reach = reach.reshape(N * TALL)
    keep = (reach >= 0)[:, None]
    padded = np.stack([np.where(keep, part[reach], 0).astype(BF16) for part in (high, low)])
    x, f = np.meshgrid(np.arange(16), np.arange(8), indexing="ij")
    near_x, near_f = np.meshgrid(np.arange(3), np.arange(8), indexing="ij")
    into = np.zeros((4, 256, 128), np.float32)
    for k in range(4):
        into[k, x * 8 + f, f * 16 + x] = 1.0
        into[k, 128 + near_x * 32 + 8 * k + near_f, near_f * 16 + near_x] = 1.0
    into = into.astype(BF16)
    back = np.transpose(into, (0, 2, 1)).copy()
    tall = padded.reshape(2, N, TALL, P_SIZE)
    return backward, padded.transpose(0, 2, 1).copy(), tall, into, back


def transposed_groups(parts, lanes):
    count = len(parts)
    group = 128 // count
    distance = count // 2
    parts = list(parts)
    while distance:
        shift = distance * group
        upper = (lanes // shift) % 2 == 1
        for q in range(count):
            if q & distance:
                continue
            a, b = parts[q], parts[q + distance]
            parts[q] = jnp.where(upper, pltpu.roll(b, shift, 1), a)
            parts[q + distance] = jnp.where(upper, b, pltpu.roll(a, 128 - shift, 1))
        distance //= 2
    return parts


def dot(a, b):
    return jnp.dot(a, b, preferred_element_type=F32)


def iota(shape, axis):
    return lax.broadcasted_iota(I32, shape, axis)


def halves(x):
    high = x.astype(BF16)
    return high, (x - high.astype(F32)).astype(BF16)


def one_hot(mask):
    return jnp.where(mask, 1.0, 0.0).astype(BF16)


def looked_up(table, places):
    return jnp.take_along_axis(table, places, axis=1)


def permuted(table, order):
    upper, lower = order >> 7, order & 127
    out = jnp.zeros((ROWS, LANES), F32)
    for k in range(ROWS):
        line = jnp.broadcast_to(table[k : k + 1, :], (ROWS, LANES))
        out = jnp.where(upper == k, looked_up(line, lower), out)
    return out


def column(line):
    eye = iota((LANES, LANES), 0) == iota((LANES, LANES), 1)
    spread = jnp.where(eye, jnp.broadcast_to(line.astype(F32), (LANES, LANES)), 0.0)
    return dot(spread.astype(BF16), jnp.ones((LANES, LANES), BF16))


def block_sums(mats, start, vec, group):
    high, low = [], []
    for n in range(32):
        part = mats[pl.ds(start, LANES), 128 * n : 128 * n + 128].astype(F32) * vec
        one, two = halves(part)
        high.append(one)
        low.append(two)
    total = jnp.zeros((256, LANES), F32)
    for q in range(4):
        cut = slice(8 * q, 8 * q + 8)
        both = jnp.concatenate(
            [jnp.concatenate(high[cut], axis=1), jnp.concatenate(low[cut], axis=1)], axis=0
        )
        total += dot(both, group[1024 * q : 1024 * q + 1024])
    return total[:LANES] + total[LANES:]


def solve_kernel(
    charges_hbm, order_hbm, anchor_hbm, pairs_hbm, project_hbm, interp_hbm, near_hbm, k_hbm,
    bwd_hbm, yfwd_hbm, ybwd_hbm, into_hbm, back_hbm,
    out_ref,
    charges, order, anchor, pairs, bwd, yfwd, ybwd, into, back, group, zline,
    pv, iv, nv, qd, cells, slots, terms, inverse,
    kv, s1, sb1, r1, hs1, hr1, sb2, r2, sb3, r3, sb4, r4, hs4, hr4, acc, nb,
    in_sem, k_sem, ns_sem, nr_sem, s1_sem, r1_sem, s2_sem, r2_sem, s3_sem, r3_sem,
    s4_sem, r4_sem, h_sem,
):
    row = lax.axis_index("row")
    col = lax.axis_index("col")
    mesh_id = pl.DeviceIdType.MESH

    def at(a, b):
        return (lax.rem(row + a + N, N), lax.rem(col + b + N, N))

    barrier = pltpu.get_barrier_semaphore()

    def greet(k, _):
        pl.semaphore_signal(barrier, inc=1, device_id=at(k, 0), device_id_type=mesh_id)
        pl.semaphore_signal(barrier, inc=1, device_id=at(0, k), device_id_type=mesh_id)
        return 0

    lax.fori_loop(1, N, greet, 0)

    def greet_beside(k, _):
        pl.semaphore_signal(barrier, inc=1, device_id=at(1, k), device_id_type=mesh_id)
        pl.semaphore_signal(barrier, inc=1, device_id=at(-1, k), device_id_type=mesh_id)
        return 0

    lax.fori_loop(1, N, greet_beside, 0)
    small = [
        pltpu.make_async_copy(src, dst, in_sem.at[3 + n])
        for n, (src, dst) in enumerate(
            [
                (order_hbm, order), (charges_hbm, charges), (anchor_hbm, anchor),
                (pairs_hbm, pairs), (bwd_hbm, bwd), (yfwd_hbm, yfwd),
                (ybwd_hbm, ybwd), (into_hbm, into), (back_hbm, back),
            ]
        )
    ]
    for copy in small[:4]:
        copy.start()
    p_copy = pltpu.make_async_copy(project_hbm, pv, in_sem.at[0])
    i_copy = pltpu.make_async_copy(interp_hbm, iv, in_sem.at[1])
    n_copy = pltpu.make_async_copy(near_hbm, nv, in_sem.at[2])
    p_copy.start()
    for copy in small[4:]:
        copy.start()
    k_copies = [
        pltpu.make_async_copy(k_hbm.at[:, pl.ds(128 * h, 128)], kv.at[h], k_sem.at[h])
        for h in range(4)
    ]
    for copy in k_copies:
        copy.start()
    n_copy.start()
    i_copy.start()

    def grouped(n, _):
        rows = pl.ds(pl.multiple_of(512 * n, 512), 512)
        group[rows] = one_hot(
            (iota((512, LANES), 0) >> 6) + 8 * n == (iota((512, LANES), 1) & (BLK - 1))
        )
        return 0

    lax.fori_loop(0, 8, grouped, 0)
    for copy in small[:4]:
        copy.wait()
    permutation = order[...]
    q_slots = permuted(charges[...].astype(F32), permutation)
    block_of = iota((LANES, ROWS), 0) >> 1
    q_rows = dot(one_hot(block_of == iota((LANES, ROWS), 1)), q_slots.astype(BF16))
    odd = (iota((LANES, LANES), 0) & 1) == 1
    right = iota((LANES, LANES), 1) >= BLK
    q_both = jnp.where(odd == right, q_rows, pltpu.roll(q_rows, BLK, 1))
    qd[...] = q_both.astype(BF16)
    p_copy.wait()
    patch = block_sums(pv, 0, q_both, group)
    for copy in small[4:]:
        copy.wait()
    x_rows = column(anchor[0:1, :] - 16 * row).astype(I32)
    y_rows = column(anchor[1:2, :] - 16 * col).astype(I32)
    z_rows = column(anchor[2:3, :]).astype(I32)
    corner = 16 * x_rows + 4 * y_rows
    lane = iota((LANES, LANES), 1)
    spot = (x_rows + (lane >> 4)) * TALL + y_rows + ((lane >> 2) & 3)
    cells[...] = jnp.where(lane < BLK, spot, 0)
    at_z = jnp.concatenate(
        [
            jnp.concatenate([one_hot(z_rows + l == lane + 128 * h) for h in range(2)], axis=1)
            for l in range(4)
        ],
        axis=0,
    )
    for n in range(2):
        zline[n] = dot(at_z, ybwd[n, :, 0:16].reshape(G, P_SIZE)).astype(BF16)
    seen, places = [], []
    for h in range(4):
        cell = iota((1, LANES), 1) + 128 * h
        cell_x = lax.div(cell, TALL)
        cell_y = cell - TALL * cell_x
        seen.append((((cell_x - x_rows) | (cell_y - y_rows)) >> 2) == 0)
        places.append((16 * cell_x + 4 * cell_y) - corner)
    weights = []
    for l in range(4):
        weights.append(
            jnp.concatenate(
                [
                    jnp.where(seen[h], looked_up(patch, (places[h] + l) & (LANES - 1)), 0.0)
                    for h in range(4)
                ],
                axis=1,
            )
        )
    high, low = halves(jnp.concatenate(weights, axis=0))

    def across(a, b):
        return lax.dot_general(a, b, (((0,), (0,)), ((), ())), preferred_element_type=F32)

    lanes = lax.broadcasted_iota(I32, (1, 128), 1)
    spread = across(high, zline[0]) + across(high, zline[1]) + across(low, zline[0])
    s1[...] = spread[0:EXT].reshape(WIDE, TALL, 512)
    for k in range(4):
        cols = slice(128 * k, 128 * k + 128)
        parts = [s1[q, :, cols] for q in range(16)]
        for q, part in enumerate(transposed_groups(parts, lanes)):
            j = q % 4
            sb1[j // 2, 4 * k + q // 4, j % 2] = part.astype(BF16)
        parts = [s1[16 + q, :, cols] for q in range(4)]
        for q, part in enumerate(transposed_groups(parts, lanes)):
            hs1[4 * k + q] = part.astype(BF16)
    pl.semaphore_wait(barrier, 4 * (N - 1))

    def remote(src, dst, send, recv, who):
        return pltpu.make_async_remote_copy(
            src_ref=src, dst_ref=dst, send_sem=send, recv_sem=recv,
            device_id=who, device_id_type=mesh_id,
        )

    def drained(ref, sem):
        pltpu.make_async_copy(ref, ref, sem).wait()

    def exchange(src, dst, me, send, recv, along):
        def one(k, _):
            to = lax.rem(me + k, N)
            who = (row, to) if along == "col" else (to, col)
            remote(src.at[to], dst.at[me], send, recv, who).start()
            return 0

        lax.fori_loop(1, N, one, 0)
        dst[me] = src[me]

    def exchange_beside(src, dst, send, recv, step):
        def one(k, _):
            to = lax.rem(col + k, N)
            who = (lax.rem(row + step + N, N), to)
            remote(src.at[to], dst.at[col], send, recv, who).start()
            return 0

        lax.fori_loop(0, N, one, 0)

    exchange(sb1.at[0], r1.at[0], col, s1_sem.at[0], r1_sem.at[0], "col")
    exchange_beside(hs1, hr1, h_sem.at[0], h_sem.at[1], 1)
    exchange(sb1.at[1], r1.at[1], col, s1_sem.at[1], r1_sem.at[1], "col")
    near_copies = []
    for k, (a, b) in enumerate(NEIGHBOURS):
        slot = NEIGHBOURS.index((-a, -b))
        near_copies.append(remote(qd, nb.at[slot], ns_sem.at[k], nr_sem.at[slot], at(a, b)))
    for copy in near_copies:
        copy.start()
    source = pairs[1:2, :]
    place = source >> 7
    slot = ((place >> 4) - row + 1) * 3 + ((place & 15) - col + 1)
    slot = jnp.where(slot == 4, 8, jnp.where(slot > 4, slot - 1, slot))
    for t in range(4):
        cut = slice(128 * t, 128 * t + 128)
        slots[t, 0:1] = slot[:, cut]
        slots[t, 1:2] = (source & 127)[:, cut]

    def second(k, _):
        drained(r1.at[k, pl.ds(0, N - 1)], r1_sem.at[k])

        @pl.when(k == 0)
        def _():
            drained(hr1, h_sem.at[1])

        lines = []
        for j in range(2):
            both = jnp.concatenate(
                [r1[k, :, j].reshape(N * TALL, 128), hr1[...].reshape(N * TALL, 128)], axis=1
            )
            lines.append(dot(both, into[2 * k + j]).astype(BF16))
        lines = jnp.concatenate(lines, axis=1)
        out = dot(yfwd[0], lines) + dot(yfwd[1], lines)
        for j in range(2):
            sb2[k, :, j] = out[:, 128 * j : 128 * j + 128].astype(BF16).reshape(N, 32, 128)
        exchange(sb2.at[k], r2.at[k], row, s2_sem.at[k], r2_sem.at[k], "row")
        return 0

    lax.fori_loop(0, CH, second, 0)
    for copy in k_copies:
        copy.wait()
    for copy in near_copies:
        copy.wait()
    n_copy.wait()

    def near_part(t):
        slot_rows = column(slots[t, 0:1]).astype(I32)
        place_rows = column(slots[t, 1:2]).astype(I32)
        lane = iota((LANES, LANES), 1)
        picked = jnp.zeros((LANES, LANES), F32)
        for s in range(9):
            table = qd[...] if s == 8 else nb[s]
            picked += dot(one_hot((slot_rows == s) & (place_rows == lane)), table)
        terms[t] = block_sums(nv, pl.multiple_of(128 * t, 128), picked, group)

    def first(k, _):
        near_part(2 * k)
        near_part(2 * k + 1)
        drained(r2.at[k, pl.ds(0, N - 1)], r2_sem.at[k])
        for j in range(2):
            sides = []
            for h in range(2):
                parts = [r2[k, 8 * h + q, j].astype(F32) for q in range(8)]
                sides.append(jnp.concatenate(transposed_groups(parts, lanes), axis=0).astype(BF16))
            lines = jnp.concatenate(sides, axis=1)
            spec = sum(dot(lines, ybwd[n, :, 0:16].reshape(G, P_SIZE)) for n in range(2))
            cols = []
            for h in range(4):
                weights = jnp.concatenate(
                    [kv[h, pl.ds(16 * k + 8 * j + q, 32, stride=32), :] for q in range(8)], axis=0
                )
                cols.append((spec[:, 128 * h : 128 * h + 128] * weights).astype(BF16))
            weighted = jnp.concatenate(cols, axis=1)
            field = dot(weighted, bwd[0]) + dot(weighted, bwd[1])
            for h in range(2):
                parts = [field[32 * q : 32 * q + 32, 128 * h : 128 * h + 128] for q in range(8)]
                for q, part in enumerate(transposed_groups(parts, lanes)):
                    sb3[k, 8 * h + q, j] = part.astype(BF16)
        exchange(sb3.at[k], r3.at[k], row, s3_sem.at[k], r3_sem.at[k], "row")
        return 0

    lax.fori_loop(0, CH, first, 0)
    near = jnp.zeros((LANES, LANES), F32)
    for t in range(4):
        target = pairs[0:1, 128 * t : 128 * t + 128] - 128 * (row * N + col)
        hot = one_hot(iota((LANES, LANES), 0) == target)
        for part in halves(terms[t]):
            near += dot(hot, part)
    terms[0] = near
    inverse[...] = jnp.zeros_like(inverse)

    def inverted(k, total):
        lines = order[pl.ds(pl.multiple_of(8 * k, 8), 8), :]
        for j in range(8):
            line = lines[j : j + 1, :]
            at_row = iota((ROWS, LANES), 0) == (line >> 7)
            both = jnp.concatenate(
                [
                    jnp.where(at_row, iota((ROWS, LANES), 1).astype(F32), 0.0),
                    jnp.where(at_row, (8 * k + j).astype(F32), 0.0),
                ],
                axis=0,
            ).astype(BF16)
            hot = one_hot(iota((LANES, LANES), 0) == (line & 127))
            total += lax.dot_general(
                both, hot, (((1,), (1,)), ((), ())), preferred_element_type=F32
            )
        return total

    acc[...] = jnp.zeros_like(acc)

    def second_back(k, _):
        def prepare(n, _):
            inverse[...] += inverted(4 * k + n, jnp.zeros((LANES, LANES), F32))
            return 0

        lax.fori_loop(0, 4, prepare, 0)
        drained(r3.at[k, pl.ds(0, N - 1)], r3_sem.at[k])
        lines = jnp.concatenate([r3[k, :, j].reshape(512, 128) for j in range(2)], axis=1)
        part = sum(dot(ybwd[n].reshape(N * TALL, P_SIZE), lines) for n in range(2)).astype(BF16)
        for j in range(2):
            moved = dot(part[:, 128 * j : 128 * j + 128], back[2 * k + j])
            sb4[k, :, j] = moved[:, 0:128].astype(BF16).reshape(N, TALL, 128)
            acc[...] += moved[:, 128:256]
        exchange(sb4.at[k], r4.at[k], col, s4_sem.at[k], r4_sem.at[k], "col")
        return 0

    lax.fori_loop(0, CH, second_back, 0)
    hs4[...] = acc[...].astype(BF16).reshape(N, TALL, 128)
    exchange_beside(hs4, hr4, h_sem.at[2], h_sem.at[3], -1)
    for k in range(CH):
        drained(sb1.at[k, pl.ds(0, N - 1)], s1_sem.at[k])
        drained(sb2.at[k, pl.ds(0, N - 1)], s2_sem.at[k])
        drained(sb3.at[k, pl.ds(0, N - 1)], s3_sem.at[k])
        drained(r4.at[k, pl.ds(0, N - 1)], r4_sem.at[k])
    drained(hs1, h_sem.at[0])
    drained(hr4, h_sem.at[3])
    for k in range(4):
        cols = slice(128 * k, 128 * k + 128)
        parts = [r4[q % 4 // 2, 4 * k + q // 4, q % 2].astype(F32) for q in range(16)]
        for q, part in enumerate(transposed_groups(parts, lanes)):
            s1[q, :, cols] = part
        parts = [hr4[4 * k + q].astype(F32) for q in range(4)]
        for q, part in enumerate(transposed_groups(parts, lanes)):
            s1[16 + q, :, cols] = part
    lines = s1[...].reshape(EXT, 512).astype(BF16)
    lines = jnp.concatenate([lines, jnp.zeros((PICK - EXT, 512), BF16)], axis=0)
    field = sum(
        lax.dot_general(zline[n], lines, (((1,), (1,)), ((), ())), preferred_element_type=F32)
        for n in range(2)
    )
    spot = cells[...]
    side, spot = spot >> 7, spot & 127
    lane = iota((LANES, LANES), 1)
    values = jnp.zeros((LANES, LANES), F32)
    for l in range(4):
        rows = field[128 * l : 128 * l + 128]
        value = looked_up(rows[:, 0:128], spot)
        for h in range(1, 4):
            value = jnp.where(side == h, looked_up(rows[:, 128 * h : 128 * h + 128], spot), value)
        values = jnp.where((lane & 3) == l, value, values)
    values = jnp.where(lane < BLK, values, 0.0).astype(BF16).astype(F32)
    values = values + pltpu.roll(values, BLK, 1)
    for k in range(CH):
        drained(sb4.at[k, pl.ds(0, N - 1)], s4_sem.at[k])
    drained(hs4, h_sem.at[2])
    i_copy.wait()

    total = block_sums(iv, 0, values, group) + terms[0]
    total = jnp.where(odd == right, total, 0.0)
    gather_rows = one_hot(iota((ROWS, LANES), 0) == (iota((ROWS, LANES), 1) >> 1))
    by_slot = sum(dot(gather_rows, part) for part in halves(total))
    back_order = inverse[...].astype(I32)
    out_ref[...] = permuted(by_slot, back_order[ROWS:] * 128 + back_order[:ROWS])


def solve(charges, order, anchor, pairs, project, interpolate, near_blocks, kernel_spectrum):
    consts = tables()
    vmem = pl.BlockSpec(memory_space=pltpu.VMEM)
    hbm = pl.BlockSpec(memory_space=pl.ANY)
    dma = pltpu.SemaphoreType.DMA
    return pl.pallas_call(
        solve_kernel,
        out_shape=jax.ShapeDtypeStruct((ROWS, LANES), F32),
        in_specs=[hbm] * 13,
        out_specs=vmem,
        scratch_shapes=[
            pltpu.VMEM((ROWS, LANES), BF16),
            pltpu.VMEM((ROWS, LANES), I32),
            pltpu.VMEM((3, LANES), I32),
            pltpu.VMEM((2, 512), I32),
            pltpu.VMEM((2, 512, 256), BF16),
            pltpu.VMEM((2, 512, N * TALL), BF16),
            pltpu.VMEM((2, N, TALL, 512), BF16),
            pltpu.VMEM((4, 256, 128), BF16),
            pltpu.VMEM((4, 128, 256), BF16),
            pltpu.VMEM((4096, LANES), BF16),
            pltpu.VMEM((2, 512, 512), BF16),
            pltpu.VMEM((128, 4096), BF16),
            pltpu.VMEM((128, 4096), BF16),
            pltpu.VMEM((512, 4096), BF16),
            pltpu.VMEM((LANES, LANES), BF16),
            pltpu.VMEM((LANES, LANES), I32),
            pltpu.VMEM((4, 8, LANES), I32),
            pltpu.VMEM((4, LANES, LANES), F32),
            pltpu.VMEM((LANES, LANES), F32),
            pltpu.VMEM((4, 1024, 128), F32),
            pltpu.VMEM((WIDE, TALL, 512), F32),
            pltpu.VMEM((CH, N, 2, TALL, 128), BF16),
            pltpu.VMEM((CH, N, 2, TALL, 128), BF16),
            pltpu.VMEM((N, TALL, 128), BF16),
            pltpu.VMEM((N, TALL, 128), BF16),
            pltpu.VMEM((CH, N, 2, 32, 128), BF16),
            pltpu.VMEM((CH, N, 2, 32, 128), BF16),
            pltpu.VMEM((CH, N, 2, 32, 128), BF16),
            pltpu.VMEM((CH, N, 2, 32, 128), BF16),
            pltpu.VMEM((CH, N, 2, TALL, 128), BF16),
            pltpu.VMEM((CH, N, 2, TALL, 128), BF16),
            pltpu.VMEM((N, TALL, 128), BF16),
            pltpu.VMEM((N, TALL, 128), BF16),
            pltpu.VMEM((N * TALL, 128), F32),
            pltpu.VMEM((8, LANES, LANES), BF16),
            dma((12,)),
            dma((4,)),
            dma((8,)),
            dma((8,)),
            dma((CH,)),
            dma((CH,)),
            dma((CH,)),
            dma((CH,)),
            dma((CH,)),
            dma((CH,)),
            dma((CH,)),
            dma((CH,)),
            dma((4,)),
        ],
        compiler_params=pltpu.CompilerParams(
            collective_id=0, has_side_effects=True, vmem_limit_bytes=62 << 20
        ),
    )(
        charges.reshape(ROWS, LANES),
        order.reshape(ROWS, LANES),
        anchor,
        pairs,
        project,
        interpolate,
        near_blocks,
        kernel_spectrum.reshape(1024, P_SIZE),
        *[jnp.asarray(part) for part in consts],
    )


def body(
    charges,
    panel_order,
    patch_anchor,
    project,
    interpolate,
    kernel_spectrum,
    near_pairs,
    near_blocks,
):
    out = solve(
        charges, panel_order, patch_anchor, near_pairs, project, interpolate, near_blocks,
        kernel_spectrum,
    )
    return out.reshape(ROWS * LANES)


def solution(mesh):
    placed = (
        P(("row", "col")),
        P(("row", "col")),
        P(None, ("row", "col")),
        P(("row", "col"), None),
        P(("row", "col"), None),
        P("row", "col", None),
        P(None, ("row", "col")),
        P(("row", "col"), None),
    )
    return jax.shard_map(
        body, mesh=mesh, in_specs=placed, out_specs=P(("row", "col")), check_vma=False
    )
```

```python
import math

import jax
import jax.numpy as jnp
import numpy as np
from jax import lax
from jax.experimental import pallas as pl
from jax.experimental.pallas import tpu as pltpu
from jax.sharding import PartitionSpec as P

G = 256
P_SIZE = 512
BLK = 64
PTS = 64
N = 16
TALL = 24
WIDE = 20
EXT = TALL * WIDE
CH = 2
F32 = jnp.float32
BF16 = jnp.bfloat16
LANES = 128
ROWS = 64
PICK = 512
I32 = jnp.int32
NEIGHBOURS = [(a, b) for a in (-1, 0, 1) for b in (-1, 0, 1) if (a, b) != (0, 0)]


def tables():
    first = np.arange(G)[:, None]
    second = np.arange(P_SIZE)[None, :]
    phase = (first * second % P_SIZE).astype(np.float64) * (2.0 * math.pi / P_SIZE)
    table = (np.cos(phase) + np.sin(phase)) / math.sqrt(P_SIZE)
    high = table.astype(BF16)
    low = (table - high.astype(np.float64)).astype(BF16)
    backward = np.stack([high.T, low.T])
    reach = np.zeros((N, TALL), np.int64) - 1
    for c in range(N):
        for y in range(19):
            if 16 * c + y < G:
                reach[c, y] = 16 * c + y
    reach = reach.reshape(N * TALL)
    keep = (reach >= 0)[:, None]
    padded = np.stack([np.where(keep, part[reach], 0).astype(BF16) for part in (high, low)])
    x, f = np.meshgrid(np.arange(16), np.arange(8), indexing="ij")
    near_x, near_f = np.meshgrid(np.arange(3), np.arange(8), indexing="ij")
    into = np.zeros((4, 256, 128), np.float32)
    for k in range(4):
        into[k, x * 8 + f, f * 16 + x] = 1.0
        into[k, 128 + near_x * 32 + 8 * k + near_f, near_f * 16 + near_x] = 1.0
    into = into.astype(BF16)
    back = np.transpose(into, (0, 2, 1)).copy()
    tall = padded.reshape(2, N, TALL, P_SIZE)
    return backward, padded.transpose(0, 2, 1).copy(), tall, into, back


def transposed_groups(parts, lanes):
    count = len(parts)
    group = 128 // count
    distance = count // 2
    parts = list(parts)
    while distance:
        shift = distance * group
        upper = (lanes // shift) % 2 == 1
        for q in range(count):
            if q & distance:
                continue
            a, b = parts[q], parts[q + distance]
            parts[q] = jnp.where(upper, pltpu.roll(b, shift, 1), a)
            parts[q + distance] = jnp.where(upper, b, pltpu.roll(a, 128 - shift, 1))
        distance //= 2
    return parts


def dot(a, b):
    return jnp.dot(a, b, preferred_element_type=F32)


def iota(shape, axis):
    return lax.broadcasted_iota(I32, shape, axis)


def halves(x):
    high = x.astype(BF16)
    return high, (x - high.astype(F32)).astype(BF16)


def one_hot(mask):
    return jnp.where(mask, 1.0, 0.0).astype(BF16)


def looked_up(table, places):
    return jnp.take_along_axis(table, places, axis=1)


def permuted(table, order):
    upper, lower = order >> 7, order & 127
    out = jnp.zeros((ROWS, LANES), F32)
    for k in range(ROWS):
        line = jnp.broadcast_to(table[k : k + 1, :], (ROWS, LANES))
        out = jnp.where(upper == k, looked_up(line, lower), out)
    return out


def column(line):
    eye = iota((LANES, LANES), 0) == iota((LANES, LANES), 1)
    spread = jnp.where(eye, jnp.broadcast_to(line.astype(F32), (LANES, LANES)), 0.0)
    return dot(spread.astype(BF16), jnp.ones((LANES, LANES), BF16))


def block_sums(mats, start, vec, group):
    high, low = [], []
    for n in range(32):
        part = mats[pl.ds(start, LANES), 128 * n : 128 * n + 128].astype(F32) * vec
        one, two = halves(part)
        high.append(one)
        low.append(two)
    total = jnp.zeros((256, LANES), F32)
    for q in range(4):
        cut = slice(8 * q, 8 * q + 8)
        both = jnp.concatenate(
            [jnp.concatenate(high[cut], axis=1), jnp.concatenate(low[cut], axis=1)], axis=0
        )
        total += dot(both, group[1024 * q : 1024 * q + 1024])
    return total[:LANES] + total[LANES:]


def solve_kernel(
    charges_hbm, order_hbm, anchor_hbm, pairs_hbm, project_hbm, interp_hbm, near_hbm, k_hbm,
    bwd_hbm, yfwd_hbm, ybwd_hbm, into_hbm, back_hbm,
    out_ref,
    charges, order, anchor, pairs, bwd, yfwd, ybwd, into, back, group, zline,
    pv, iv, nv, qd, cells, slots, terms, inverse,
    kv, s1, sb1, r1, hs1, hr1, sb2, r2, sb3, r3, sb4, r4, hs4, hr4, acc, nb,
    in_sem, k_sem, ns_sem, nr_sem, s1_sem, r1_sem, s2_sem, r2_sem, s3_sem, r3_sem,
    s4_sem, r4_sem, h_sem,
):
    row = lax.axis_index("row")
    col = lax.axis_index("col")
    mesh_id = pl.DeviceIdType.MESH

    def at(a, b):
        return (lax.rem(row + a + N, N), lax.rem(col + b + N, N))

    small = [
        pltpu.make_async_copy(src, dst, in_sem.at[3 + n])
        for n, (src, dst) in enumerate(
            [
                (order_hbm, order), (charges_hbm, charges), (anchor_hbm, anchor),
                (pairs_hbm, pairs), (bwd_hbm, bwd), (yfwd_hbm, yfwd),
                (ybwd_hbm, ybwd), (into_hbm, into), (back_hbm, back),
            ]
        )
    ]
    for copy in small[:4]:
        copy.start()
    p_copy = pltpu.make_async_copy(project_hbm, pv, in_sem.at[0])
    i_copy = pltpu.make_async_copy(interp_hbm, iv, in_sem.at[1])
    n_copy = pltpu.make_async_copy(near_hbm, nv, in_sem.at[2])
    p_copy.start()
    for copy in small[4:]:
        copy.start()
    barrier = pltpu.get_barrier_semaphore()

    def greet(k, _):
        pl.semaphore_signal(barrier, inc=1, device_id=at(k, 0), device_id_type=mesh_id)
        pl.semaphore_signal(barrier, inc=1, device_id=at(0, k), device_id_type=mesh_id)
        return 0

    lax.fori_loop(1, N, greet, 0)

    def greet_beside(k, _):
        pl.semaphore_signal(barrier, inc=1, device_id=at(1, k), device_id_type=mesh_id)
        pl.semaphore_signal(barrier, inc=1, device_id=at(-1, k), device_id_type=mesh_id)
        return 0

    lax.fori_loop(1, N, greet_beside, 0)
    k_copies = [
        pltpu.make_async_copy(k_hbm.at[:, pl.ds(128 * h, 128)], kv.at[h], k_sem.at[h])
        for h in range(4)
    ]
    def grouped(n, _):
        rows = pl.ds(pl.multiple_of(512 * n, 512), 512)
        group[rows] = one_hot(
            (iota((512, LANES), 0) >> 6) + 8 * n == (iota((512, LANES), 1) & (BLK - 1))
        )
        return 0

    lax.fori_loop(0, 8, grouped, 0)
    for copy in small[:4]:
        copy.wait()
    permutation = order[...]
    q_slots = permuted(charges[...].astype(F32), permutation)
    block_of = iota((LANES, ROWS), 0) >> 1
    q_rows = dot(one_hot(block_of == iota((LANES, ROWS), 1)), q_slots.astype(BF16))
    odd = (iota((LANES, LANES), 0) & 1) == 1
    right = iota((LANES, LANES), 1) >= BLK
    q_both = jnp.where(odd == right, q_rows, pltpu.roll(q_rows, BLK, 1))
    qd[...] = q_both.astype(BF16)
    p_copy.wait()
    patch = block_sums(pv, 0, q_both, group)
    for copy in small[4:]:
        copy.wait()
    for copy in k_copies:
        copy.start()
    n_copy.start()
    i_copy.start()
    x_rows = column(anchor[0:1, :] - 16 * row).astype(I32)
    y_rows = column(anchor[1:2, :] - 16 * col).astype(I32)
    z_rows = column(anchor[2:3, :]).astype(I32)
    corner = 16 * x_rows + 4 * y_rows
    lane = iota((LANES, LANES), 1)
    spot = (x_rows + (lane >> 4)) * TALL + y_rows + ((lane >> 2) & 3)
    cells[...] = jnp.where(lane < BLK, spot, 0)
    at_z = jnp.concatenate(
        [
            jnp.concatenate([one_hot(z_rows + l == lane + 128 * h) for h in range(2)], axis=1)
            for l in range(4)
        ],
        axis=0,
    )
    for n in range(2):
        zline[n] = dot(at_z, ybwd[n, :, 0:16].reshape(G, P_SIZE)).astype(BF16)
    seen, places = [], []
    for h in range(4):
        cell = iota((1, LANES), 1) + 128 * h
        cell_x = lax.div(cell, TALL)
        cell_y = cell - TALL * cell_x
        seen.append((((cell_x - x_rows) | (cell_y - y_rows)) >> 2) == 0)
        places.append((16 * cell_x + 4 * cell_y) - corner)
    weights = []
    for l in range(4):
        weights.append(
            jnp.concatenate(
                [
                    jnp.where(seen[h], looked_up(patch, (places[h] + l) & (LANES - 1)), 0.0)
                    for h in range(4)
                ],
                axis=1,
            )
        )
    high, low = halves(jnp.concatenate(weights, axis=0))

    def across(a, b):
        return lax.dot_general(a, b, (((0,), (0,)), ((), ())), preferred_element_type=F32)

    lanes = lax.broadcasted_iota(I32, (1, 128), 1)
    spread = across(high, jnp.concatenate([zline[0], zline[1]], axis=1))
    spread = spread[:, 0:512] + spread[:, 512:1024] + across(low, zline[0])
    s1[...] = spread[0:EXT].reshape(WIDE, TALL, 512)
    for k in range(4):
        cols = slice(128 * k, 128 * k + 128)
        parts = [s1[q, :, cols] for q in range(16)]
        for q, part in enumerate(transposed_groups(parts, lanes)):
            j = q % 4
            sb1[j // 2, 4 * k + q // 4, j % 2] = part.astype(BF16)
        parts = [s1[16 + q, :, cols] for q in range(4)]
        for q, part in enumerate(transposed_groups(parts, lanes)):
            hs1[4 * k + q] = part.astype(BF16)
    pl.semaphore_wait(barrier, 4 * (N - 1))

    def remote(src, dst, send, recv, who):
        return pltpu.make_async_remote_copy(
            src_ref=src, dst_ref=dst, send_sem=send, recv_sem=recv,
            device_id=who, device_id_type=mesh_id,
        )

    def drained(ref, sem):
        pltpu.make_async_copy(ref, ref, sem).wait()

    def exchange(src, dst, me, send, recv, along):
        def one(k, _):
            to = lax.rem(me + k, N)
            who = (row, to) if along == "col" else (to, col)
            remote(src.at[to], dst.at[me], send, recv, who).start()
            return 0

        lax.fori_loop(1, N, one, 0)
        dst[me] = src[me]

    def exchange_beside(src, dst, send, recv, step):
        def one(k, _):
            to = lax.rem(col + k, N)
            who = (lax.rem(row + step + N, N), to)
            remote(src.at[to], dst.at[col], send, recv, who).start()
            return 0

        lax.fori_loop(0, N, one, 0)

    exchange_beside(hs1, hr1, h_sem.at[0], h_sem.at[1], 1)
    exchange(sb1.at[0], r1.at[0], col, s1_sem.at[0], r1_sem.at[0], "col")
    exchange(sb1.at[1], r1.at[1], col, s1_sem.at[1], r1_sem.at[1], "col")
    near_copies = []
    for k, (a, b) in enumerate(NEIGHBOURS):
        slot = NEIGHBOURS.index((-a, -b))
        near_copies.append(remote(qd, nb.at[slot], ns_sem.at[k], nr_sem.at[slot], at(a, b)))
    for copy in near_copies:
        copy.start()
    source = pairs[1:2, :]
    place = source >> 7
    slot = ((place >> 4) - row + 1) * 3 + ((place & 15) - col + 1)
    slot = jnp.where(slot == 4, 8, jnp.where(slot > 4, slot - 1, slot))
    for t in range(4):
        cut = slice(128 * t, 128 * t + 128)
        slots[t, 0:1] = slot[:, cut]
        slots[t, 1:2] = (source & 127)[:, cut]

    def second(k, _):
        drained(r1.at[k, pl.ds(0, N - 1)], r1_sem.at[k])

        @pl.when(k == 0)
        def _():
            drained(hr1, h_sem.at[1])

        lines = []
        for j in range(2):
            both = jnp.concatenate(
                [r1[k, :, j].reshape(N * TALL, 128), hr1[...].reshape(N * TALL, 128)], axis=1
            )
            lines.append(dot(both, into[2 * k + j]).astype(BF16))
        lines = jnp.concatenate(lines, axis=1)
        out = dot(yfwd[0], lines) + dot(yfwd[1], lines)
        for j in range(2):
            sb2[k, :, j] = out[:, 128 * j : 128 * j + 128].astype(BF16).reshape(N, 32, 128)
        exchange(sb2.at[k], r2.at[k], row, s2_sem.at[k], r2_sem.at[k], "row")
        return 0

    lax.fori_loop(0, CH, second, 0)
    for copy in k_copies:
        copy.wait()
    for copy in near_copies:
        copy.wait()
    n_copy.wait()

    def near_part(t):
        slot_rows = column(slots[t, 0:1]).astype(I32)
        place_rows = column(slots[t, 1:2]).astype(I32)
        lane = iota((LANES, LANES), 1)
        picked = jnp.zeros((LANES, LANES), F32)
        for s in range(9):
            table = qd[...] if s == 8 else nb[s]
            picked += dot(one_hot((slot_rows == s) & (place_rows == lane)), table)
        terms[t] = block_sums(nv, pl.multiple_of(128 * t, 128), picked, group)

    def first(k, _):
        near_part(2 * k)
        near_part(2 * k + 1)
        drained(r2.at[k, pl.ds(0, N - 1)], r2_sem.at[k])
        for j in range(2):
            sides = []
            for h in range(2):
                parts = [r2[k, 8 * h + q, j].astype(F32) for q in range(8)]
                sides.append(jnp.concatenate(transposed_groups(parts, lanes), axis=0).astype(BF16))
            lines = jnp.concatenate(sides, axis=1)
            spec = sum(dot(lines, ybwd[n, :, 0:16].reshape(G, P_SIZE)) for n in range(2))
            cols = []
            for h in range(4):
                weights = jnp.concatenate(
                    [kv[h, pl.ds(16 * k + 8 * j + q, 32, stride=32), :] for q in range(8)], axis=0
                )
                cols.append((spec[:, 128 * h : 128 * h + 128] * weights).astype(BF16))
            weighted = jnp.concatenate(cols, axis=1)
            field = dot(weighted, bwd[0]) + dot(weighted, bwd[1])
            for h in range(2):
                parts = [field[32 * q : 32 * q + 32, 128 * h : 128 * h + 128] for q in range(8)]
                for q, part in enumerate(transposed_groups(parts, lanes)):
                    sb3[k, 8 * h + q, j] = part.astype(BF16)
        exchange(sb3.at[k], r3.at[k], row, s3_sem.at[k], r3_sem.at[k], "row")
        return 0

    lax.fori_loop(0, CH, first, 0)
    near = jnp.zeros((LANES, LANES), F32)
    for t in range(4):
        target = pairs[0:1, 128 * t : 128 * t + 128] - 128 * (row * N + col)
        hot = one_hot(iota((LANES, LANES), 0) == target)
        for part in halves(terms[t]):
            near += dot(hot, part)
    terms[0] = near
    inverse[...] = jnp.zeros_like(inverse)

    def inverted(k, total):
        lines = order[pl.ds(pl.multiple_of(8 * k, 8), 8), :]
        for j in range(8):
            line = lines[j : j + 1, :]
            at_row = iota((ROWS, LANES), 0) == (line >> 7)
            both = jnp.concatenate(
                [
                    jnp.where(at_row, iota((ROWS, LANES), 1).astype(F32), 0.0),
                    jnp.where(at_row, (8 * k + j).astype(F32), 0.0),
                ],
                axis=0,
            ).astype(BF16)
            hot = one_hot(iota((LANES, LANES), 0) == (line & 127))
            total += lax.dot_general(
                both, hot, (((1,), (1,)), ((), ())), preferred_element_type=F32
            )
        return total

    acc[...] = jnp.zeros_like(acc)

    def second_back(k, _):
        def prepare(n, _):
            inverse[...] += inverted(4 * k + n, jnp.zeros((LANES, LANES), F32))
            return 0

        lax.fori_loop(0, 4, prepare, 0)
        drained(r3.at[k, pl.ds(0, N - 1)], r3_sem.at[k])
        lines = jnp.concatenate([r3[k, :, j].reshape(512, 128) for j in range(2)], axis=1)
        part = sum(dot(ybwd[n].reshape(N * TALL, P_SIZE), lines) for n in range(2)).astype(BF16)
        for j in range(2):
            moved = dot(part[:, 128 * j : 128 * j + 128], back[2 * k + j])
            sb4[k, :, j] = moved[:, 0:128].astype(BF16).reshape(N, TALL, 128)
            acc[...] += moved[:, 128:256]
        exchange(sb4.at[k], r4.at[k], col, s4_sem.at[k], r4_sem.at[k], "col")
        return 0

    lax.fori_loop(0, CH, second_back, 0)
    hs4[...] = acc[...].astype(BF16).reshape(N, TALL, 128)
    exchange_beside(hs4, hr4, h_sem.at[2], h_sem.at[3], -1)
    for k in range(CH):
        drained(sb1.at[k, pl.ds(0, N - 1)], s1_sem.at[k])
        drained(sb2.at[k, pl.ds(0, N - 1)], s2_sem.at[k])
        drained(sb3.at[k, pl.ds(0, N - 1)], s3_sem.at[k])
        drained(r4.at[k, pl.ds(0, N - 1)], r4_sem.at[k])
    drained(hs1, h_sem.at[0])
    drained(hr4, h_sem.at[3])
    for k in range(4):
        cols = slice(128 * k, 128 * k + 128)
        parts = [r4[q % 4 // 2, 4 * k + q // 4, q % 2].astype(F32) for q in range(16)]
        for q, part in enumerate(transposed_groups(parts, lanes)):
            s1[q, :, cols] = part
        parts = [hr4[4 * k + q].astype(F32) for q in range(4)]
        for q, part in enumerate(transposed_groups(parts, lanes)):
            s1[16 + q, :, cols] = part
    lines = s1[...].reshape(EXT, 512).astype(BF16)
    lines = jnp.concatenate([lines, jnp.zeros((PICK - EXT, 512), BF16)], axis=0)
    field = sum(
        lax.dot_general(zline[n], lines, (((1,), (1,)), ((), ())), preferred_element_type=F32)
        for n in range(2)
    )
    spot = cells[...]
    side, spot = spot >> 7, spot & 127
    lane = iota((LANES, LANES), 1)
    values = jnp.zeros((LANES, LANES), F32)
    for l in range(4):
        rows = field[128 * l : 128 * l + 128]
        value = looked_up(rows[:, 0:128], spot)
        for h in range(1, 4):
            value = jnp.where(side == h, looked_up(rows[:, 128 * h : 128 * h + 128], spot), value)
        values = jnp.where((lane & 3) == l, value, values)
    values = jnp.where(lane < BLK, values, 0.0).astype(BF16).astype(F32)
    values = values + pltpu.roll(values, BLK, 1)
    for k in range(CH):
        drained(sb4.at[k, pl.ds(0, N - 1)], s4_sem.at[k])
    drained(hs4, h_sem.at[2])
    i_copy.wait()

    total = block_sums(iv, 0, values, group) + terms[0]
    total = jnp.where(odd == right, total, 0.0)
    gather_rows = one_hot(iota((ROWS, LANES), 0) == (iota((ROWS, LANES), 1) >> 1))
    by_slot = sum(dot(gather_rows, part) for part in halves(total))
    back_order = inverse[...].astype(I32)
    out_ref[...] = permuted(by_slot, back_order[ROWS:] * 128 + back_order[:ROWS])


def solve(charges, order, anchor, pairs, project, interpolate, near_blocks, kernel_spectrum):
    consts = tables()
    vmem = pl.BlockSpec(memory_space=pltpu.VMEM)
    hbm = pl.BlockSpec(memory_space=pl.ANY)
    dma = pltpu.SemaphoreType.DMA
    return pl.pallas_call(
        solve_kernel,
        out_shape=jax.ShapeDtypeStruct((ROWS, LANES), F32),
        in_specs=[hbm] * 13,
        out_specs=vmem,
        scratch_shapes=[
            pltpu.VMEM((ROWS, LANES), BF16),
            pltpu.VMEM((ROWS, LANES), I32),
            pltpu.VMEM((3, LANES), I32),
            pltpu.VMEM((2, 512), I32),
            pltpu.VMEM((2, 512, 256), BF16),
            pltpu.VMEM((2, 512, N * TALL), BF16),
            pltpu.VMEM((2, N, TALL, 512), BF16),
            pltpu.VMEM((4, 256, 128), BF16),
            pltpu.VMEM((4, 128, 256), BF16),
            pltpu.VMEM((4096, LANES), BF16),
            pltpu.VMEM((2, 512, 512), BF16),
            pltpu.VMEM((128, 4096), BF16),
            pltpu.VMEM((128, 4096), BF16),
            pltpu.VMEM((512, 4096), BF16),
            pltpu.VMEM((LANES, LANES), BF16),
            pltpu.VMEM((LANES, LANES), I32),
            pltpu.VMEM((4, 8, LANES), I32),
            pltpu.VMEM((4, LANES, LANES), F32),
            pltpu.VMEM((LANES, LANES), F32),
            pltpu.VMEM((4, 1024, 128), F32),
            pltpu.VMEM((WIDE, TALL, 512), F32),
            pltpu.VMEM((CH, N, 2, TALL, 128), BF16),
            pltpu.VMEM((CH, N, 2, TALL, 128), BF16),
            pltpu.VMEM((N, TALL, 128), BF16),
            pltpu.VMEM((N, TALL, 128), BF16),
            pltpu.VMEM((CH, N, 2, 32, 128), BF16),
            pltpu.VMEM((CH, N, 2, 32, 128), BF16),
            pltpu.VMEM((CH, N, 2, 32, 128), BF16),
            pltpu.VMEM((CH, N, 2, 32, 128), BF16),
            pltpu.VMEM((CH, N, 2, TALL, 128), BF16),
            pltpu.VMEM((CH, N, 2, TALL, 128), BF16),
            pltpu.VMEM((N, TALL, 128), BF16),
            pltpu.VMEM((N, TALL, 128), BF16),
            pltpu.VMEM((N * TALL, 128), F32),
            pltpu.VMEM((8, LANES, LANES), BF16),
            dma((12,)),
            dma((4,)),
            dma((8,)),
            dma((8,)),
            dma((CH,)),
            dma((CH,)),
            dma((CH,)),
            dma((CH,)),
            dma((CH,)),
            dma((CH,)),
            dma((CH,)),
            dma((CH,)),
            dma((4,)),
        ],
        compiler_params=pltpu.CompilerParams(
            collective_id=0, has_side_effects=True, vmem_limit_bytes=62 << 20
        ),
    )(
        charges.reshape(ROWS, LANES),
        order.reshape(ROWS, LANES),
        anchor,
        pairs,
        project,
        interpolate,
        near_blocks,
        kernel_spectrum.reshape(1024, P_SIZE),
        *[jnp.asarray(part) for part in consts],
    )


def body(
    charges,
    panel_order,
    patch_anchor,
    project,
    interpolate,
    kernel_spectrum,
    near_pairs,
    near_blocks,
):
    out = solve(
        charges, panel_order, patch_anchor, near_pairs, project, interpolate, near_blocks,
        kernel_spectrum,
    )
    return out.reshape(ROWS * LANES)


def solution(mesh):
    placed = (
        P(("row", "col")),
        P(("row", "col")),
        P(None, ("row", "col")),
        P(("row", "col"), None),
        P(("row", "col"), None),
        P("row", "col", None),
        P(None, ("row", "col")),
        P(("row", "col"), None),
    )
    return jax.shard_map(
        body, mesh=mesh, in_specs=placed, out_specs=P(("row", "col")), check_vma=False
    )
```

```python
import math

import jax
import jax.numpy as jnp
import numpy as np
from jax import lax
from jax.experimental import pallas as pl
from jax.experimental.pallas import tpu as pltpu
from jax.sharding import PartitionSpec as P

G = 256
P_SIZE = 512
BLK = 64
PTS = 64
N = 16
TALL = 24
WIDE = 20
EXT = TALL * WIDE
CH = 2
F32 = jnp.float32
BF16 = jnp.bfloat16
LANES = 128
ROWS = 64
PICK = 512
I32 = jnp.int32
NEIGHBOURS = [(a, b) for a in (-1, 0, 1) for b in (-1, 0, 1) if (a, b) != (0, 0)]


def tables():
    first = np.arange(G)[:, None]
    second = np.arange(P_SIZE)[None, :]
    phase = (first * second % P_SIZE).astype(np.float64) * (2.0 * math.pi / P_SIZE)
    table = (np.cos(phase) + np.sin(phase)) / math.sqrt(P_SIZE)
    high = table.astype(BF16)
    low = (table - high.astype(np.float64)).astype(BF16)
    backward = np.stack([high.T, low.T])
    reach = np.zeros((N, TALL), np.int64) - 1
    for c in range(N):
        for y in range(19):
            if 16 * c + y < G:
                reach[c, y] = 16 * c + y
    reach = reach.reshape(N * TALL)
    keep = (reach >= 0)[:, None]
    padded = np.stack([np.where(keep, part[reach], 0).astype(BF16) for part in (high, low)])
    x, f = np.meshgrid(np.arange(16), np.arange(8), indexing="ij")
    near_x, near_f = np.meshgrid(np.arange(3), np.arange(8), indexing="ij")
    into = np.zeros((4, 256, 128), np.float32)
    for k in range(4):
        into[k, x * 8 + f, f * 16 + x] = 1.0
        into[k, 128 + near_x * 32 + 8 * k + near_f, near_f * 16 + near_x] = 1.0
    into = into.astype(BF16)
    back = np.transpose(into, (0, 2, 1)).copy()
    tall = padded.reshape(2, N, TALL, P_SIZE)
    return backward, padded.transpose(0, 2, 1).copy(), tall, into, back


def transposed_groups(parts, lanes):
    count = len(parts)
    group = 128 // count
    distance = count // 2
    parts = list(parts)
    while distance:
        shift = distance * group
        upper = (lanes // shift) % 2 == 1
        for q in range(count):
            if q & distance:
                continue
            a, b = parts[q], parts[q + distance]
            parts[q] = jnp.where(upper, pltpu.roll(b, shift, 1), a)
            parts[q + distance] = jnp.where(upper, b, pltpu.roll(a, 128 - shift, 1))
        distance //= 2
    return parts


def dot(a, b):
    return jnp.dot(a, b, preferred_element_type=F32)


def iota(shape, axis):
    return lax.broadcasted_iota(I32, shape, axis)


def halves(x):
    high = x.astype(BF16)
    return high, (x - high.astype(F32)).astype(BF16)


def one_hot(mask):
    return jnp.where(mask, 1.0, 0.0).astype(BF16)


def looked_up(table, places):
    return jnp.take_along_axis(table, places, axis=1)


def permuted(table, order):
    upper, lower = order >> 7, order & 127
    out = jnp.zeros((ROWS, LANES), F32)
    for k in range(ROWS):
        line = jnp.broadcast_to(table[k : k + 1, :], (ROWS, LANES))
        out = jnp.where(upper == k, looked_up(line, lower), out)
    return out


def column(line):
    eye = iota((LANES, LANES), 0) == iota((LANES, LANES), 1)
    spread = jnp.where(eye, jnp.broadcast_to(line.astype(F32), (LANES, LANES)), 0.0)
    return dot(spread.astype(BF16), jnp.ones((LANES, LANES), BF16))


def block_sums(mats, start, vec, group):
    high, low = [], []
    for n in range(32):
        part = mats[pl.ds(start, LANES), 128 * n : 128 * n + 128].astype(F32) * vec
        one, two = halves(part)
        high.append(one)
        low.append(two)
    total = jnp.zeros((256, LANES), F32)
    for q in range(4):
        cut = slice(8 * q, 8 * q + 8)
        both = jnp.concatenate(
            [jnp.concatenate(high[cut], axis=1), jnp.concatenate(low[cut], axis=1)], axis=0
        )
        total += dot(both, group[1024 * q : 1024 * q + 1024])
    return total[:LANES] + total[LANES:]


def solve_kernel(
    charges_hbm, order_hbm, anchor_hbm, pairs_hbm, project_hbm, interp_hbm, near_hbm, k_hbm,
    bwd_hbm, yfwd_hbm, ybwd_hbm, into_hbm, back_hbm,
    out_ref,
    charges, order, anchor, pairs, bwd, yfwd, ybwd, into, back, group, zline,
    pv, iv, nv, qd, cells, slots, terms, inverse,
    kv, s1, sb1, r1, hs1, hr1, sb2, r2, sb3, r3, sb4, r4, hs4, hr4, acc, nb,
    in_sem, k_sem, ns_sem, nr_sem, s1_sem, r1_sem, s2_sem, r2_sem, s3_sem, r3_sem,
    s4_sem, r4_sem, h_sem,
):
    row = lax.axis_index("row")
    col = lax.axis_index("col")
    mesh_id = pl.DeviceIdType.MESH

    def at(a, b):
        return (lax.rem(row + a + N, N), lax.rem(col + b + N, N))

    small = [
        pltpu.make_async_copy(src, dst, in_sem.at[3 + n])
        for n, (src, dst) in enumerate(
            [
                (order_hbm, order), (charges_hbm, charges), (anchor_hbm, anchor),
                (pairs_hbm, pairs), (bwd_hbm, bwd), (yfwd_hbm, yfwd),
                (ybwd_hbm, ybwd), (into_hbm, into), (back_hbm, back),
            ]
        )
    ]
    for copy in small[:4]:
        copy.start()
    p_copy = pltpu.make_async_copy(project_hbm, pv, in_sem.at[0])
    i_copy = pltpu.make_async_copy(interp_hbm, iv, in_sem.at[1])
    n_copy = pltpu.make_async_copy(near_hbm, nv, in_sem.at[2])
    p_copy.start()
    for copy in small[4:]:
        copy.start()
    barrier = pltpu.get_barrier_semaphore()

    def greet(k, _):
        pl.semaphore_signal(barrier, inc=1, device_id=at(k, 0), device_id_type=mesh_id)
        pl.semaphore_signal(barrier, inc=1, device_id=at(0, k), device_id_type=mesh_id)
        return 0

    lax.fori_loop(1, N, greet, 0)

    def greet_beside(k, _):
        pl.semaphore_signal(barrier, inc=1, device_id=at(1, k), device_id_type=mesh_id)
        pl.semaphore_signal(barrier, inc=1, device_id=at(-1, k), device_id_type=mesh_id)
        return 0

    lax.fori_loop(1, N, greet_beside, 0)
    k_copies = [
        pltpu.make_async_copy(k_hbm.at[:, pl.ds(128 * h, 128)], kv.at[h], k_sem.at[h])
        for h in range(4)
    ]
    def grouped(n, _):
        rows = pl.ds(pl.multiple_of(512 * n, 512), 512)
        group[rows] = one_hot(
            (iota((512, LANES), 0) >> 6) + 8 * n == (iota((512, LANES), 1) & (BLK - 1))
        )
        return 0

    lax.fori_loop(0, 8, grouped, 0)
    for copy in small[:4]:
        copy.wait()
    permutation = order[...]
    q_slots = permuted(charges[...].astype(F32), permutation)
    block_of = iota((LANES, ROWS), 0) >> 1
    q_rows = dot(one_hot(block_of == iota((LANES, ROWS), 1)), q_slots.astype(BF16))
    odd = (iota((LANES, LANES), 0) & 1) == 1
    right = iota((LANES, LANES), 1) >= BLK
    q_both = jnp.where(odd == right, q_rows, pltpu.roll(q_rows, BLK, 1))
    qd[...] = q_both.astype(BF16)
    p_copy.wait()
    patch = block_sums(pv, 0, q_both, group)
    for copy in small[4:]:
        copy.wait()
    for copy in k_copies:
        copy.start()
    n_copy.start()
    i_copy.start()
    x_rows = column(anchor[0:1, :] - 16 * row).astype(I32)
    y_rows = column(anchor[1:2, :] - 16 * col).astype(I32)
    z_rows = column(anchor[2:3, :]).astype(I32)
    corner = 16 * x_rows + 4 * y_rows
    lane = iota((LANES, LANES), 1)
    spot = (x_rows + (lane >> 4)) * TALL + y_rows + ((lane >> 2) & 3)
    cells[...] = jnp.where(lane < BLK, spot, 0)
    at_z = jnp.concatenate(
        [
            jnp.concatenate([one_hot(z_rows + l == lane + 128 * h) for h in range(2)], axis=1)
            for l in range(4)
        ],
        axis=0,
    )
    for n in range(2):
        zline[n] = dot(at_z, ybwd[n, :, 0:16].reshape(G, P_SIZE)).astype(BF16)
    seen, places = [], []
    for h in range(4):
        cell = iota((1, LANES), 1) + 128 * h
        cell_x = lax.div(cell, TALL)
        cell_y = cell - TALL * cell_x
        seen.append((((cell_x - x_rows) | (cell_y - y_rows)) >> 2) == 0)
        places.append((16 * cell_x + 4 * cell_y) - corner)
    weights = []
    for l in range(4):
        weights.append(
            jnp.concatenate(
                [
                    jnp.where(seen[h], looked_up(patch, (places[h] + l) & (LANES - 1)), 0.0)
                    for h in range(4)
                ],
                axis=1,
            )
        )
    high, low = halves(jnp.concatenate(weights, axis=0))

    def across(a, b):
        return lax.dot_general(a, b, (((0,), (0,)), ((), ())), preferred_element_type=F32)

    lanes = lax.broadcasted_iota(I32, (1, 128), 1)
    spread = across(high, jnp.concatenate([zline[0], zline[1]], axis=1))
    spread = spread[:, 0:512] + spread[:, 512:1024] + across(low, zline[0])
    s1[...] = spread[0:EXT].reshape(WIDE, TALL, 512)
    for k in range(4):
        cols = slice(128 * k, 128 * k + 128)
        parts = [s1[q, :, cols] for q in range(16)]
        for q, part in enumerate(transposed_groups(parts, lanes)):
            j = q % 4
            sb1[j // 2, 4 * k + q // 4, j % 2] = part.astype(BF16)
        parts = [s1[16 + q, :, cols] for q in range(4)]
        for q, part in enumerate(transposed_groups(parts, lanes)):
            hs1[4 * k + q] = part.astype(BF16)
    pl.semaphore_wait(barrier, 4 * (N - 1))

    def remote(src, dst, send, recv, who):
        return pltpu.make_async_remote_copy(
            src_ref=src, dst_ref=dst, send_sem=send, recv_sem=recv,
            device_id=who, device_id_type=mesh_id,
        )

    def drained(ref, sem):
        pltpu.make_async_copy(ref, ref, sem).wait()

    def exchange(src, dst, me, send, recv, along):
        def one(k, _):
            to = lax.rem(me + k, N)
            who = (row, to) if along == "col" else (to, col)
            remote(src.at[to], dst.at[me], send, recv, who).start()
            return 0

        lax.fori_loop(1, N, one, 0)
        dst[me] = src[me]

    def exchange_beside(src, dst, send, recv, step):
        def one(k, _):
            to = lax.rem(col + k, N)
            who = (lax.rem(row + step + N, N), to)
            remote(src.at[to], dst.at[col], send, recv, who).start()
            return 0

        lax.fori_loop(0, N, one, 0)

    exchange_beside(hs1, hr1, h_sem.at[0], h_sem.at[1], 1)
    exchange(sb1.at[0], r1.at[0], col, s1_sem.at[0], r1_sem.at[0], "col")
    exchange(sb1.at[1], r1.at[1], col, s1_sem.at[1], r1_sem.at[1], "col")
    near_copies = []
    for k, (a, b) in enumerate(NEIGHBOURS):
        slot = NEIGHBOURS.index((-a, -b))
        near_copies.append(remote(qd, nb.at[slot], ns_sem.at[k], nr_sem.at[slot], at(a, b)))
    for copy in near_copies:
        copy.start()
    source = pairs[1:2, :]
    place = source >> 7
    slot = ((place >> 4) - row + 1) * 3 + ((place & 15) - col + 1)
    slot = jnp.where(slot == 4, 8, jnp.where(slot > 4, slot - 1, slot))
    for t in range(4):
        cut = slice(128 * t, 128 * t + 128)
        slots[t, 0:1] = slot[:, cut]
        slots[t, 1:2] = (source & 127)[:, cut]

    def second(k, _):
        drained(r1.at[k, pl.ds(0, N - 1)], r1_sem.at[k])

        @pl.when(k == 0)
        def _():
            drained(hr1, h_sem.at[1])

        lines = []
        for j in range(2):
            both = jnp.concatenate(
                [r1[k, :, j].reshape(N * TALL, 128), hr1[...].reshape(N * TALL, 128)], axis=1
            )
            lines.append(dot(both, into[2 * k + j]).astype(BF16))
        lines = jnp.concatenate(lines, axis=1)
        out = dot(yfwd[0], lines) + dot(yfwd[1], lines)
        for j in range(2):
            sb2[k, :, j] = out[:, 128 * j : 128 * j + 128].astype(BF16).reshape(N, 32, 128)
        exchange(sb2.at[k], r2.at[k], row, s2_sem.at[k], r2_sem.at[k], "row")
        return 0

    lax.fori_loop(0, CH, second, 0)
    for copy in k_copies:
        copy.wait()
    for copy in near_copies:
        copy.wait()
    n_copy.wait()

    def near_part(t):
        slot_rows = column(slots[t, 0:1]).astype(I32)
        place_rows = column(slots[t, 1:2]).astype(I32)
        lane = iota((LANES, LANES), 1)
        picked = jnp.zeros((LANES, LANES), F32)
        for s in range(9):
            table = qd[...] if s == 8 else nb[s]
            picked += dot(one_hot((slot_rows == s) & (place_rows == lane)), table)
        terms[t] = block_sums(nv, pl.multiple_of(128 * t, 128), picked, group)

    def first(k, _):
        near_part(2 * k)
        near_part(2 * k + 1)
        drained(r2.at[k, pl.ds(0, N - 1)], r2_sem.at[k])
        for j in range(2):
            sides = []
            for h in range(2):
                parts = [r2[k, 8 * h + q, j].astype(F32) for q in range(8)]
                sides.append(jnp.concatenate(transposed_groups(parts, lanes), axis=0).astype(BF16))
            lines = jnp.concatenate(sides, axis=1)
            spec = sum(dot(lines, ybwd[n, :, 0:16].reshape(G, P_SIZE)) for n in range(2))
            cols = []
            for h in range(4):
                weights = jnp.concatenate(
                    [kv[h, pl.ds(16 * k + 8 * j + q, 32, stride=32), :] for q in range(8)], axis=0
                )
                cols.append((spec[:, 128 * h : 128 * h + 128] * weights).astype(BF16))
            weighted = jnp.concatenate(cols, axis=1)
            field = dot(weighted, bwd[0]) + dot(weighted, bwd[1])
            for h in range(2):
                parts = [field[32 * q : 32 * q + 32, 128 * h : 128 * h + 128] for q in range(8)]
                for q, part in enumerate(transposed_groups(parts, lanes)):
                    sb3[k, 8 * h + q, j] = part.astype(BF16)

            def send_half(n, _, j=j):
                to = lax.rem(row + n, N)
                remote(
                    sb3.at[k, to, j], r3.at[k, row, j], s3_sem.at[k], r3_sem.at[k], (to, col)
                ).start()
                return 0

            lax.fori_loop(1, N, send_half, 0)
        r3[k, row] = sb3[k, row]
        return 0

    lax.fori_loop(0, CH, first, 0)
    near = jnp.zeros((LANES, LANES), F32)
    for t in range(4):
        target = pairs[0:1, 128 * t : 128 * t + 128] - 128 * (row * N + col)
        hot = one_hot(iota((LANES, LANES), 0) == target)
        for part in halves(terms[t]):
            near += dot(hot, part)
    terms[0] = near
    inverse[...] = jnp.zeros_like(inverse)

    def inverted(k, total):
        lines = order[pl.ds(pl.multiple_of(8 * k, 8), 8), :]
        for j in range(8):
            line = lines[j : j + 1, :]
            at_row = iota((ROWS, LANES), 0) == (line >> 7)
            both = jnp.concatenate(
                [
                    jnp.where(at_row, iota((ROWS, LANES), 1).astype(F32), 0.0),
                    jnp.where(at_row, (8 * k + j).astype(F32), 0.0),
                ],
                axis=0,
            ).astype(BF16)
            hot = one_hot(iota((LANES, LANES), 0) == (line & 127))
            total += lax.dot_general(
                both, hot, (((1,), (1,)), ((), ())), preferred_element_type=F32
            )
        return total

    acc[...] = jnp.zeros_like(acc)

    def second_back(k, _):
        def prepare(n, _):
            inverse[...] += inverted(4 * k + n, jnp.zeros((LANES, LANES), F32))
            return 0

        lax.fori_loop(0, 4, prepare, 0)
        drained(r3.at[k, pl.ds(0, N - 1)], r3_sem.at[k])
        lines = jnp.concatenate([r3[k, :, j].reshape(512, 128) for j in range(2)], axis=1)
        part = sum(dot(ybwd[n].reshape(N * TALL, P_SIZE), lines) for n in range(2)).astype(BF16)
        for j in range(2):
            moved = dot(part[:, 128 * j : 128 * j + 128], back[2 * k + j])
            sb4[k, :, j] = moved[:, 0:128].astype(BF16).reshape(N, TALL, 128)
            acc[...] += moved[:, 128:256]
        exchange(sb4.at[k], r4.at[k], col, s4_sem.at[k], r4_sem.at[k], "col")
        return 0

    lax.fori_loop(0, CH, second_back, 0)
    hs4[...] = acc[...].astype(BF16).reshape(N, TALL, 128)
    exchange_beside(hs4, hr4, h_sem.at[2], h_sem.at[3], -1)
    for k in range(CH):
        drained(sb1.at[k, pl.ds(0, N - 1)], s1_sem.at[k])
        drained(sb2.at[k, pl.ds(0, N - 1)], s2_sem.at[k])
        drained(sb3.at[k, pl.ds(0, N - 1)], s3_sem.at[k])
        drained(r4.at[k, pl.ds(0, N - 1)], r4_sem.at[k])
    drained(hs1, h_sem.at[0])
    drained(hr4, h_sem.at[3])
    for k in range(4):
        cols = slice(128 * k, 128 * k + 128)
        parts = [r4[q % 4 // 2, 4 * k + q // 4, q % 2].astype(F32) for q in range(16)]
        for q, part in enumerate(transposed_groups(parts, lanes)):
            s1[q, :, cols] = part
        parts = [hr4[4 * k + q].astype(F32) for q in range(4)]
        for q, part in enumerate(transposed_groups(parts, lanes)):
            s1[16 + q, :, cols] = part
    lines = s1[...].reshape(EXT, 512).astype(BF16)
    lines = jnp.concatenate([lines, jnp.zeros((PICK - EXT, 512), BF16)], axis=0)
    field = sum(
        lax.dot_general(zline[n], lines, (((1,), (1,)), ((), ())), preferred_element_type=F32)
        for n in range(2)
    )
    spot = cells[...]
    side, spot = spot >> 7, spot & 127
    lane = iota((LANES, LANES), 1)
    values = jnp.zeros((LANES, LANES), F32)
    for l in range(4):
        rows = field[128 * l : 128 * l + 128]
        value = looked_up(rows[:, 0:128], spot)
        for h in range(1, 4):
            value = jnp.where(side == h, looked_up(rows[:, 128 * h : 128 * h + 128], spot), value)
        values = jnp.where((lane & 3) == l, value, values)
    values = jnp.where(lane < BLK, values, 0.0).astype(BF16).astype(F32)
    values = values + pltpu.roll(values, BLK, 1)
    for k in range(CH):
        drained(sb4.at[k, pl.ds(0, N - 1)], s4_sem.at[k])
    drained(hs4, h_sem.at[2])
    i_copy.wait()

    total = block_sums(iv, 0, values, group) + terms[0]
    total = jnp.where(odd == right, total, 0.0)
    gather_rows = one_hot(iota((ROWS, LANES), 0) == (iota((ROWS, LANES), 1) >> 1))
    by_slot = sum(dot(gather_rows, part) for part in halves(total))
    back_order = inverse[...].astype(I32)
    out_ref[...] = permuted(by_slot, back_order[ROWS:] * 128 + back_order[:ROWS])


def solve(charges, order, anchor, pairs, project, interpolate, near_blocks, kernel_spectrum):
    consts = tables()
    vmem = pl.BlockSpec(memory_space=pltpu.VMEM)
    hbm = pl.BlockSpec(memory_space=pl.ANY)
    dma = pltpu.SemaphoreType.DMA
    return pl.pallas_call(
        solve_kernel,
        out_shape=jax.ShapeDtypeStruct((ROWS, LANES), F32),
        in_specs=[hbm] * 13,
        out_specs=vmem,
        scratch_shapes=[
            pltpu.VMEM((ROWS, LANES), BF16),
            pltpu.VMEM((ROWS, LANES), I32),
            pltpu.VMEM((3, LANES), I32),
            pltpu.VMEM((2, 512), I32),
            pltpu.VMEM((2, 512, 256), BF16),
            pltpu.VMEM((2, 512, N * TALL), BF16),
            pltpu.VMEM((2, N, TALL, 512), BF16),
            pltpu.VMEM((4, 256, 128), BF16),
            pltpu.VMEM((4, 128, 256), BF16),
            pltpu.VMEM((4096, LANES), BF16),
            pltpu.VMEM((2, 512, 512), BF16),
            pltpu.VMEM((128, 4096), BF16),
            pltpu.VMEM((128, 4096), BF16),
            pltpu.VMEM((512, 4096), BF16),
            pltpu.VMEM((LANES, LANES), BF16),
            pltpu.VMEM((LANES, LANES), I32),
            pltpu.VMEM((4, 8, LANES), I32),
            pltpu.VMEM((4, LANES, LANES), F32),
            pltpu.VMEM((LANES, LANES), F32),
            pltpu.VMEM((4, 1024, 128), F32),
            pltpu.VMEM((WIDE, TALL, 512), F32),
            pltpu.VMEM((CH, N, 2, TALL, 128), BF16),
            pltpu.VMEM((CH, N, 2, TALL, 128), BF16),
            pltpu.VMEM((N, TALL, 128), BF16),
            pltpu.VMEM((N, TALL, 128), BF16),
            pltpu.VMEM((CH, N, 2, 32, 128), BF16),
            pltpu.VMEM((CH, N, 2, 32, 128), BF16),
            pltpu.VMEM((CH, N, 2, 32, 128), BF16),
            pltpu.VMEM((CH, N, 2, 32, 128), BF16),
            pltpu.VMEM((CH, N, 2, TALL, 128), BF16),
            pltpu.VMEM((CH, N, 2, TALL, 128), BF16),
            pltpu.VMEM((N, TALL, 128), BF16),
            pltpu.VMEM((N, TALL, 128), BF16),
            pltpu.VMEM((N * TALL, 128), F32),
            pltpu.VMEM((8, LANES, LANES), BF16),
            dma((12,)),
            dma((4,)),
            dma((8,)),
            dma((8,)),
            dma((CH,)),
            dma((CH,)),
            dma((CH,)),
            dma((CH,)),
            dma((CH,)),
            dma((CH,)),
            dma((CH,)),
            dma((CH,)),
            dma((4,)),
        ],
        compiler_params=pltpu.CompilerParams(
            collective_id=0, has_side_effects=True, vmem_limit_bytes=62 << 20
        ),
    )(
        charges.reshape(ROWS, LANES),
        order.reshape(ROWS, LANES),
        anchor,
        pairs,
        project,
        interpolate,
        near_blocks,
        kernel_spectrum.reshape(1024, P_SIZE),
        *[jnp.asarray(part) for part in consts],
    )


def body(
    charges,
    panel_order,
    patch_anchor,
    project,
    interpolate,
    kernel_spectrum,
    near_pairs,
    near_blocks,
):
    out = solve(
        charges, panel_order, patch_anchor, near_pairs, project, interpolate, near_blocks,
        kernel_spectrum,
    )
    return out.reshape(ROWS * LANES)


def solution(mesh):
    placed = (
        P(("row", "col")),
        P(("row", "col")),
        P(None, ("row", "col")),
        P(("row", "col"), None),
        P(("row", "col"), None),
        P("row", "col", None),
        P(None, ("row", "col")),
        P(("row", "col"), None),
    )
    return jax.shard_map(
        body, mesh=mesh, in_specs=placed, out_specs=P(("row", "col")), check_vma=False
    )
```
